128 devices in a mesh: visit: 32 (over x, y, z_lo), tx: 2 (over core), ty: 2 (over z_hi).
Axes of the slice: x: 4, y: 4, z: 4 (z_hi: 2, z_lo: 2; z = z_hi * 2 + z_lo), core: 2. Of those that a mesh axis runs over, the one named last changes fastest.
Arguments:
- images: bfloat16 [32, 16, 128, 768], P('visit', None, 'ty', 'tx'), may hold values from -8 to 8
- partners: int32 [32, 16, 2], replicated, may hold values from 0 to 31, all different within a row; in each aligned block of 16 rows (0 to 15, 16 to 31, ..., all dimensions but the last counted through in order) at most 2 rows name the same one
- coverage: int32 [32, 16, 2, 16, 96], P('visit', None, None, 'ty', 'tx'), may hold values from 0 to 1, as said below
- x_filters: bfloat16 [40, 21], replicated, may hold values from -0.359375 to 0.359375
- row_filters: bfloat16 [40, 21], replicated, may hold values from -0.359375 to 0.359375
Outputs:
- coefficients: float32 [32, 16, 2, 40], P('visit', ('tx', 'ty'))
The draws below stay inside these ranges and needn't reach their ends.
Inputs may be any that keep to these rules, and one draw needn't show every extreme that they name: In the 16 rows of one visit no visit is named more than 2 times, and in some visit's rows one visit is named exactly 2 times; the two partners of a tile differ. `coverage`: each mask is 1 on one rectangle of blocks that holds the tile's last block row and last block column, and 0 elsewhere.
All inputs are finite; a program needn't handle non-finite values.
Results may differ from the reference program's by a relative error of at most 0.00065.
Values may be sent and summed in bfloat16 or wider, within the bound.
A program may use at most 64 MiB of HBM per device.

```python
import math
import jax
import jax.numpy as jnp
import numpy as np
from jax import lax

K = 40
TAPS = 21
CAP = 2
BLK = 8
VISITS = 32
TILES = 16
HEIGHT = 128
WIDTH = 768


def blur_field(field, row_taps, col_taps):
    padded = jnp.pad(field, ((0, 0), (0, 0), (2, 2), (0, 0)))
    across = jnp.zeros(field.shape, jnp.float32)
    for tap_index in range(5):
        across = across + row_taps[:, tap_index, None, None, None] * padded[:, :, tap_index:tap_index + HEIGHT, :]
    padded = jnp.pad(across, ((0, 0), (0, 0), (0, 0), (2, 2)))
    result = jnp.zeros(field.shape, jnp.float32)
    for tap_index in range(5):
        result = result + col_taps[:, tap_index, None, None, None] * padded[:, :, :, tap_index:tap_index + WIDTH]
    return result


def draw_images(key, part):
    sky_key = jax.random.fold_in(key, 101)
    sky = jax.random.normal(sky_key, (TILES, HEIGHT, WIDTH), jnp.float32)
    center = jnp.where(jnp.arange(5) == 2, 1.0, 0.0).astype(jnp.float32)
    first_taps = center[None, None, :] + 0.35 * jax.random.normal(jax.random.fold_in(key, 102), (VISITS, 2, 5), jnp.float32)
    second_taps = center[None, None, :] + 0.35 * jax.random.normal(jax.random.fold_in(key, 103), (VISITS, 2, 5), jnp.float32)
    field = jnp.broadcast_to(sky[None], (VISITS, TILES, HEIGHT, WIDTH))
    ramp = (jnp.arange(HEIGHT, dtype=jnp.float32)[:, None] + jnp.arange(WIDTH, dtype=jnp.float32)[None, :]) / (HEIGHT + WIDTH - 2.0)
    mixed = (1.0 - ramp) * blur_field(field, first_taps[:, 0], first_taps[:, 1]) + ramp * blur_field(field, second_taps[:, 0], second_taps[:, 1])
    noise = 0.3 * jax.random.normal(jax.random.fold_in(key, 104), (VISITS, TILES, HEIGHT, WIDTH), jnp.float32)
    return jnp.clip(mixed + noise, -8.0, 8.0).astype(jnp.bfloat16)


def draw_coverage(key, part):
    block_rows = HEIGHT // BLK
    block_cols = WIDTH // BLK
    start_rows = jax.random.randint(jax.random.fold_in(key, 201), (VISITS, TILES, 2, 1, 1), 0, block_rows)
    start_cols = jax.random.randint(jax.random.fold_in(key, 202), (VISITS, TILES, 2, 1, 1), 0, block_cols)
    inside = (jnp.arange(block_rows)[:, None] >= start_rows) & (jnp.arange(block_cols)[None, :] >= start_cols)
    return inside.astype(jnp.int32)


def deal_out(stream_key, own, number, rows, number_of, top, bound, lean):
    sequence = jax.random.permutation(stream_key, number_of)
    packed, ordinary = shares(number_of, rows * top, bound, lean, True), shares(number_of, rows * top, bound, lean, False)
    places = jnp.arange(number_of)

    def named(sizes, turn):
        used = int((sizes > 0).sum())
        fixed = max(1, used // 4)
        shifted = fixed + (places - fixed + turn * (used - fixed)) % max(1, number_of - fixed)
        return jnp.zeros((number_of,), jnp.int32).at[sequence[jnp.where(places < fixed, places, shifted)]].set(jnp.asarray(sizes, jnp.int32))

    sizes = jnp.where(number % 4 == 0, named(packed, number // 4), named(ordinary, number - number // 4 - 1))
    mixed = jax.random.permutation(jax.random.fold_in(own, 3), number_of)
    source_of, taker = mixed[0:number_of // 2 * 2:2], mixed[1:number_of // 2 * 2:2]
    room = jnp.minimum(sizes[source_of] - 1, bound - sizes[taker]) // 2
    room = jnp.where((source_of == sequence[0]) | (taker == sequence[0]) | (sizes[taker] == 0), 0, jnp.maximum(room, 0))
    shifted = jax.random.randint(jax.random.fold_in(own, 4), (number_of // 2,), 0, 1 << 20) % (room + 1)
    sizes = sizes.at[source_of].add(-shifted).at[taker].add(shifted)
    items = jnp.searchsorted(jnp.cumsum(sizes), jnp.arange(rows * top), side="right").astype(jnp.int32)
    grid = items.reshape(top, rows).T
    grid = grid[jax.random.permutation(jax.random.fold_in(own, 1), rows)]
    turn = jax.random.randint(jax.random.fold_in(own, 2), (rows, 1), 0, top)
    return jnp.take_along_axis(grid, (jnp.arange(top)[None, :] + turn) % top, axis=1)


def shares(count, total, reach, lean, full):
    weights = [(1 << 20) // math.isqrt(grade ** lean) + 1 for grade in range(1, count + 1)]
    largest = reach if full else min(reach, max(-(-total // count), total * weights[0] // sum(weights)))
    least = 1 if total - largest >= count - 1 else 0
    holding, spare = [largest] + [least] * (count - 1), total - largest - least * (count - 1)
    while spare > 0:
        candidates = [i for i in range(1, count) if holding[i] < largest] or [i for i in range(1, count) if holding[i] < reach]
        pool, left = sum([weights[i] for i in candidates]), spare
        for i in candidates:
            addition = min(reach - holding[i], max(1, left * weights[i] // pool), spare)
            holding[i] = holding[i] + addition
            spare = spare - addition
    return np.array(holding)


def normal_values(key, extent, scale, reach, kind=jnp.bfloat16):
    return jnp.clip(scale * jax.random.normal(key, extent, jnp.float32), -reach, reach).astype(kind)


def setup_inputs(seed: int = 0) -> dict:
    arg_keys = jax.random.split(jax.random.key(seed), 6)
    images = draw_images(jax.random.fold_in(arg_keys[5], 71), 0)
    partners_keys = jax.random.split(jax.random.fold_in(arg_keys[1], 1), VISITS * TILES // TILES)
    partners_turns = jax.random.permutation(jax.random.fold_in(arg_keys[1], 3), VISITS * TILES // TILES)
    partners = jax.vmap(lambda own, number: deal_out(jax.random.fold_in(arg_keys[1], 2), own, number, TILES, VISITS, 2, CAP, 2))(partners_keys, partners_turns).reshape((VISITS, TILES, 2))
    coverage = draw_coverage(jax.random.fold_in(arg_keys[5], 71), 0)
    x_filters = normal_values(arg_keys[3], (K, TAPS), 0.06, 0.359375)
    row_filters = normal_values(arg_keys[4], (K, TAPS), 0.06, 0.359375)
    return dict(images=images, partners=partners, coverage=coverage, x_filters=x_filters, row_filters=row_filters)


RIDGE_TERM = 0.002

def solve_systems(sums, pixel_values):
    kernel_total = sums.shape[-1] - 1
    matrix = sums[..., :kernel_total, :kernel_total] / pixel_values + RIDGE_TERM * jnp.eye(kernel_total, dtype=sums.dtype)
    right_side = sums[..., :kernel_total, kernel_total] / pixel_values
    factor = jnp.linalg.cholesky(matrix)
    return jax.scipy.linalg.cho_solve((factor, True), right_side[..., None])[..., 0]

def convolve_tile(images_tile, x_filters, row_filters):
    half_width = (TAPS - 1) // 2
    field = images_tile.astype(jnp.float32)
    visit_count, height_count, width_count = field.shape
    x_values = x_filters.astype(jnp.float32)
    y_values = row_filters.astype(jnp.float32)
    padded = jnp.pad(field, ((0, 0), (0, 0), (half_width, half_width)))
    smooth = jnp.zeros((visit_count, K, height_count, width_count), jnp.float32)
    for tap_index in range(TAPS):
        smooth = smooth + x_values[None, :, tap_index, None, None] * padded[:, None, :, tap_index:tap_index + width_count]
    smooth = lax.optimization_barrier(smooth.astype(jnp.bfloat16)).astype(jnp.float32)
    padded_rows = jnp.pad(smooth, ((0, 0), (0, 0), (half_width, half_width), (0, 0)))
    basis_images = jnp.zeros((visit_count, K, height_count, width_count), jnp.float32)
    for tap_index in range(TAPS):
        basis_images = basis_images + y_values[None, :, tap_index, None, None] * padded_rows[:, :, tap_index:tap_index + height_count, :]
    return basis_images.astype(jnp.bfloat16)

def reference(images, partners, coverage, x_filters, row_filters):
    visit_count = images.shape[0]
    pixel_values = HEIGHT * WIDTH

    def per_tile(tile_index):
        basis_images = convolve_tile(images[:, tile_index], x_filters, row_filters)

        def per_visit(visit_index):
            sources = partners[visit_index, tile_index]
            templates = basis_images[sources].astype(jnp.float32)
            science = images[visit_index, tile_index].astype(jnp.float32)
            stacked = jnp.concatenate([templates, jnp.broadcast_to(science[None, None], (2, 1, HEIGHT, WIDTH))], axis=1)
            stacked = stacked.reshape(2, K + 1, HEIGHT * WIDTH)
            blocks = coverage[visit_index, tile_index]
            weights = jnp.repeat(jnp.repeat(blocks, BLK, axis=1), BLK, axis=2).astype(jnp.float32).reshape(2, 1, HEIGHT * WIDTH)
            sums = jnp.einsum('jip,jlp->jil', stacked * weights, stacked, precision=lax.Precision.HIGHEST)
            return solve_systems(sums, pixel_values)
        return lax.map(per_visit, jnp.arange(visit_count, dtype=jnp.int32))
    result = lax.map(per_tile, jnp.arange(TILES, dtype=jnp.int32))
    return jnp.transpose(result, (1, 0, 2, 3))
```

```python
import functools

import jax
import jax.numpy as jnp
from jax import lax
from jax.experimental import pallas as pl
from jax.experimental.pallas import tpu as pltpu
from jax.sharding import PartitionSpec as P

CAP = 2
RIDGE_TERM = 0.002
NT = (((1,), (1,)), ((), ()))
VMEM = pltpu.VMEM
ANY = pl.ANY


def outgoing_tiles(requests, sender_visit, tile_count):
    is_sender = (requests == sender_visit).astype(jnp.int32)
    before = jnp.cumsum(is_sender, axis=1) - is_sender
    tile_ids = jnp.arange(2 * tile_count, dtype=jnp.int32)[None, :] // 2
    picked = [
        jnp.sum(jnp.where((is_sender == 1) & (before == slot), tile_ids, 0), axis=1)
        for slot in range(CAP)
    ]
    return jnp.stack(picked, axis=1).reshape(-1)


def arrival_slots(sources):
    count = sources.shape[0]
    same_source = sources[:, None] == sources[None, :]
    earlier = jnp.arange(count)[None, :] < jnp.arange(count)[:, None]
    return sources * CAP + jnp.sum((same_source & earlier).astype(jnp.int32), axis=1)


def send_pack_kernel(index_ref, tiles_ref, out_ref, sems):
    slots = out_ref.shape[0]

    def copy(slot):
        return pltpu.make_async_copy(
            tiles_ref.at[index_ref[slot]], out_ref.at[slot], sems.at[slot]
        )

    for slot in range(slots):
        copy(slot).start()
    for slot in range(slots):
        copy(slot).wait()


def send_pack(indices, tiles):
    slots = indices.shape[0]
    return pl.pallas_call(
        send_pack_kernel,
        out_shape=jax.ShapeDtypeStruct((slots,) + tiles.shape[1:], tiles.dtype),
        grid_spec=pltpu.PrefetchScalarGridSpec(
            num_scalar_prefetch=1,
            grid=(1,),
            in_specs=[pl.BlockSpec(tiles.shape, lambda i, s: (0, 0, 0))],
            out_specs=pl.BlockSpec(memory_space=ANY),
            scratch_shapes=[pltpu.SemaphoreType.DMA((slots,))],
        ),
    )(indices, tiles)


def group_pack_kernel(index_ref, arrived_ref, tiles_ref, out_ref, sems):
    owners, per_owner = out_ref.shape[0], out_ref.shape[1]
    science = tiles_ref.shape[0] // owners
    systems = per_owner - science
    copies = []
    for owner in range(owners):
        for place in range(systems):
            copies.append((arrived_ref.at[index_ref[owner * systems + place]], owner, place))
        for place in range(science):
            copies.append((tiles_ref.at[owner * science + place], owner, systems + place))
    started = []
    for number, (source, owner, place) in enumerate(copies):
        copy = pltpu.make_async_copy(source, out_ref.at[owner, place], sems.at[number])
        copy.start()
        started.append(copy)
    for copy in started:
        copy.wait()


def group_pack(indices, arrived, tiles, owners):
    tile_count = tiles.shape[0]
    per_owner = 3 * tile_count // owners
    shape = (owners, per_owner) + tiles.shape[1:]
    return pl.pallas_call(
        group_pack_kernel,
        out_shape=jax.ShapeDtypeStruct(shape, tiles.dtype),
        grid_spec=pltpu.PrefetchScalarGridSpec(
            num_scalar_prefetch=1,
            grid=(1,),
            in_specs=[pl.BlockSpec(memory_space=ANY), pl.BlockSpec(memory_space=ANY)],
            out_specs=pl.BlockSpec(shape, lambda i, s: (0, 0, 0, 0)),
            scratch_shapes=[pltpu.SemaphoreType.DMA((3 * tile_count,))],
        ),
    )(indices, arrived, tiles)


def horizontal_table(x_filters, block_cols, span):
    taps = x_filters.shape[1]
    offsets = jnp.arange(span)[None, :] - jnp.arange(block_cols)[:, None]
    total = jnp.zeros((x_filters.shape[0], block_cols, span), jnp.bfloat16)
    for tap in range(taps):
        total = jnp.where(offsets[None] == tap, x_filters[:, tap][:, None, None], total)
    return total.reshape(-1, span)


def vertical_table(row_filters, row_count, half_width):
    kernels, taps = row_filters.shape
    offsets = jnp.arange(row_count)[:, None] - jnp.arange(row_count)[None, :] + half_width
    table = jnp.zeros((kernels, row_count, row_count), jnp.bfloat16)
    for tap in range(taps):
        table = jnp.where(offsets[None] == tap, row_filters[:, tap][:, None, None], table)
    table = table.reshape(kernels // 2, 2, row_count, row_count)
    zero = jnp.zeros_like(table[:, 0])
    upper = jnp.concatenate([table[:, 0], zero], axis=2)
    lower = jnp.concatenate([zero, table[:, 1]], axis=2)
    return jnp.concatenate([upper, lower], axis=1)


def full_tile(ref):
    upper = jnp.concatenate([ref[0, 0], ref[2, 0]], axis=1)
    lower = jnp.concatenate([ref[1, 0], ref[3, 0]], axis=1)
    return jnp.concatenate([upper, lower], axis=0)


def normals_kernel(
    half_width, bounds_ref, template_ref, science_ref, xtab_ref, ytab_ref, out_ref,
    window, stack, mask, first, second, third,
):
    system = pl.program_id(0)
    row_start, col_start = bounds_ref[2 * system], bounds_ref[2 * system + 1]
    rows, cols = 2 * template_ref.shape[2], 2 * template_ref.shape[3]
    pairs = ytab_ref.shape[0]
    kernel_total = 2 * pairs
    span = 2 * rows
    groups = span // 16
    template = full_tile(template_ref).astype(jnp.float32)
    padded = jnp.concatenate([template, jnp.zeros((rows, span), jnp.float32)], axis=1)
    window[...] = pltpu.roll(padded, half_width, axis=1).astype(jnp.bfloat16)
    first[...] = jnp.zeros_like(first)
    second[...] = jnp.zeros_like(second)
    third[...] = jnp.zeros_like(third)
    science = full_tile(science_ref)
    ones = (
        lax.broadcasted_iota(jnp.int32, (span, span), 0)
        == lax.broadcasted_iota(jnp.int32, (span, span), 1)
    ).astype(jnp.bfloat16)
    low, high = 16 * 16, 32 * 16

    def put(kernel_rows, values):
        for group in range(groups):
            stack[kernel_rows, group * rows : (group + 1) * rows] = values[group * 16 : group * 16 + 16]

    for part in range(cols // span):

        @pl.when((part + 1) * span > col_start)
        def _():
            start = part * span
            c = lax.broadcasted_iota(jnp.int32, (span, span), 0) + start
            a = lax.broadcasted_iota(jnp.int32, (span, span), 1) % rows
            mask[...] = ((c >= col_start) & (a >= row_start)).astype(jnp.bfloat16)
            put(
                slice(kernel_total * 16, kernel_total * 16 + 16),
                lax.dot_general(
                    ones, science[:, start : start + span], NT, preferred_element_type=jnp.float32
                ).astype(jnp.bfloat16) * mask[:, :rows],
            )

            def body(pair, carry):
                data = jnp.concatenate(
                    [window[:, start : start + span], window[:, start + rows : start + rows + span]], axis=0
                )
                smooth = lax.dot_general(
                    xtab_ref[pl.ds(pl.multiple_of(pair * span, span), span), :],
                    data, NT, preferred_element_type=jnp.float32,
                ).astype(jnp.bfloat16)
                moved = jnp.concatenate(
                    [
                        jnp.concatenate([smooth[:rows, :rows], smooth[rows:, :rows]], axis=1),
                        jnp.concatenate([smooth[:rows, rows:], smooth[rows:, rows:]], axis=1),
                    ],
                    axis=0,
                )
                basis = jnp.dot(moved, ytab_ref[pair], preferred_element_type=jnp.float32)
                basis = basis.astype(jnp.bfloat16) * mask[...]
                base = pl.multiple_of(pair * 32, 32)
                put(pl.ds(base, 16), basis[:, :rows])
                put(pl.ds(base + 16, 16), basis[:, rows:])
                return carry

            lax.fori_loop(0, pairs, body, 0, unroll=2)

            def gram(lhs, rhs):
                return lax.dot_general(lhs, rhs, NT, preferred_element_type=jnp.float32)

            first[:low] += gram(stack[:low], stack[:low])
            first[low:] += gram(stack[high:], stack[:low])
            second[...] += gram(stack[...], stack[low:high])
            third[...] += gram(stack[high:], stack[high:])

    def fold(ref):
        height, width = ref.shape
        r = lax.broadcasted_iota(jnp.int32, (height, width), 0)
        l = lax.broadcasted_iota(jnp.int32, (height, width), 1)
        kept = jnp.where((r % 16) == (l % 16), ref[...], 0.0)
        summed = jnp.sum(kept.reshape(height // 16, 16, width), axis=1)
        s = lax.broadcasted_iota(jnp.int32, (width, 128), 0)
        t = lax.broadcasted_iota(jnp.int32, (width, 128), 1)
        return jnp.dot(
            summed, ((s // 16) == t).astype(jnp.float32),
            preferred_element_type=jnp.float32, precision=lax.Precision.HIGHEST,
        )

    out_ref[0, 0:25] = fold(first)
    out_ref[0, 32:73] = fold(second)
    out_ref[0, 80:89] = fold(third)


def normals(bounds, gathered, xtab, ytab, half_width):
    owners, per_owner, half_rows, half_cols = gathered.shape
    systems = 2 * per_owner // 3
    rows, cols = 2 * half_rows, 2 * half_cols
    span = 2 * rows
    quarter = (owners, 1, half_rows, half_cols)
    kernel_total = 2 * ytab.shape[0]
    tall = 16 * (kernel_total + 1)
    return pl.pallas_call(
        functools.partial(normals_kernel, half_width),
        out_shape=jax.ShapeDtypeStruct((systems, 96, 128), jnp.float32),
        grid_spec=pltpu.PrefetchScalarGridSpec(
            num_scalar_prefetch=1,
            grid=(systems,),
            in_specs=[
                pl.BlockSpec(quarter, lambda i, s: (0, i, 0, 0)),
                pl.BlockSpec(quarter, lambda i, s: (0, systems + i // 2, 0, 0)),
                pl.BlockSpec(xtab.shape, lambda i, s: (0, 0)),
                pl.BlockSpec(ytab.shape, lambda i, s: (0, 0, 0)),
            ],
            out_specs=pl.BlockSpec((1, 96, 128), lambda i, s: (i, 0, 0)),
            scratch_shapes=[
                VMEM((rows, cols + span), jnp.bfloat16),
                VMEM((tall, 16 * rows), jnp.bfloat16),
                VMEM((span, span), jnp.bfloat16),
                VMEM((256 + tall - 512, 256), jnp.float32),
                VMEM((tall, 256), jnp.float32),
                VMEM((tall - 512, tall - 512), jnp.float32),
            ],
        ),
        compiler_params=pltpu.CompilerParams(vmem_limit_bytes=56 * 1024 * 1024),
    )(bounds, gathered, gathered, xtab, ytab)


def solve_kernel(kernel_total, pixel_values, blocks_ref, out_ref):
    systems = blocks_ref.shape[0]
    r = lax.broadcasted_iota(jnp.int32, (128, 128), 0)
    l = lax.broadcasted_iota(jnp.int32, (128, 128), 1)
    matrices = []
    for system in range(systems):
        blocks = blocks_ref[system]
        first, second, third = blocks[0:32], blocks[32:80], blocks[80:96]
        zero = jnp.zeros((16, 128), jnp.float32)
        left = jnp.concatenate([first[:16], zero, first[16:32]] + [zero] * 5, axis=0)
        middle = jnp.concatenate([pltpu.roll(second, 16, axis=1)] + [zero] * 5, axis=0)
        right = jnp.concatenate([zero, zero, pltpu.roll(third, 32, axis=1)] + [zero] * 5, axis=0)
        left = jnp.where((l < 16) & ((r < 16) | ((r >= 32) & (r <= kernel_total))), left, 0.0)
        middle = jnp.where((l >= 16) & (l < 32) & (r <= kernel_total), middle, 0.0)
        right = jnp.where((l >= 32) & (l <= kernel_total) & (r >= 32) & (r <= kernel_total), right, 0.0)
        known = left + middle + right
        other = jnp.transpose(known)
        absent = ((r >= 16) & (r < 32) & (l < 16)) | ((l >= 32) & (r < 32))
        whole = jnp.where(absent, other, known) / pixel_values
        whole = whole + jnp.where((r == l) & (r < kernel_total), RIDGE_TERM, 0.0)
        matrices.append(whole[:kernel_total])
    work = jnp.stack(matrices, axis=0)
    row_ids = lax.broadcasted_iota(jnp.int32, (1, kernel_total, 1), 1)
    for pivot in range(kernel_total):
        row = work[:, pivot : pivot + 1, :]
        row = row / row[:, :, pivot : pivot + 1]
        column = work[:, :, pivot : pivot + 1]
        work = jnp.where(row_ids == pivot, row, work - column * row)
    lanes = lax.broadcasted_iota(jnp.int32, work.shape, 2)
    out_ref[...] = jnp.sum(jnp.where(lanes == kernel_total, work, 0.0), axis=2)


def solve(blocks, kernel_total, pixel_values):
    return pl.pallas_call(
        functools.partial(solve_kernel, kernel_total, float(pixel_values)),
        out_shape=jax.ShapeDtypeStruct((blocks.shape[0], kernel_total), jnp.float32),
    )(blocks)


def body(images, partners, coverage, x_filters, row_filters):
    visit = lax.axis_index("visit")
    own_tiles = images[0]
    tile_count, row_count, col_count = own_tiles.shape
    half_width = (x_filters.shape[1] - 1) // 2
    kernel_total = x_filters.shape[0]
    visit_count = partners.shape[0]
    owners = lax.axis_size("tx") * lax.axis_size("ty")
    requests = partners.reshape(visit_count, 2 * tile_count)
    own_requests = lax.dynamic_index_in_dim(requests, visit, 0, keepdims=False)
    sent = send_pack(outgoing_tiles(requests, visit, tile_count), own_tiles)
    arrived = lax.all_to_all(
        sent.reshape((visit_count, CAP) + own_tiles.shape[1:]), "visit", split_axis=0, concat_axis=0, tiled=True
    )
    arrived = arrived.reshape((visit_count * CAP,) + own_tiles.shape[1:])
    grouped = group_pack(arrival_slots(own_requests), arrived, own_tiles, owners)
    gathered = lax.all_to_all(grouped, ("tx", "ty"), split_axis=0, concat_axis=0, tiled=True)

    blocks = coverage[0]
    block_size = row_count // blocks.shape[2]
    row_blocks = jnp.max(blocks, axis=3).sum(axis=2)
    col_blocks = jnp.max(blocks, axis=2).sum(axis=2)
    counts = jnp.stack([row_blocks, col_blocks], axis=-1).astype(jnp.float32)
    counts = lax.all_to_all(
        counts.reshape(owners, 2 * tile_count // owners, 2), ("tx", "ty"), split_axis=0, concat_axis=0, tiled=True
    )
    row_start = 2 * row_count - block_size * (counts[2, :, 0] + counts[3, :, 0])
    col_start = 2 * col_count - block_size * (counts[1, :, 1] + counts[3, :, 1])
    bounds = jnp.stack([row_start, col_start], axis=-1).astype(jnp.int32).reshape(-1)

    xtab = horizontal_table(x_filters, 2 * row_count, 4 * row_count)
    ytab = vertical_table(row_filters, 2 * row_count, half_width)
    sums = normals(bounds, gathered, xtab, ytab, half_width)
    pixel_values = row_count * col_count * owners
    coefficients = solve(sums, kernel_total, pixel_values)
    return coefficients.reshape(1, tile_count // owners, 2, kernel_total)


def solution(mesh):
    return jax.shard_map(
        body,
        mesh=mesh,
        in_specs=(P("visit", None, "ty", "tx"), P(), P("visit", None, None, "ty", "tx"), P(), P()),
        out_specs=P("visit", ("tx", "ty"), None, None),
        check_vma=False,
    )
```

```python
import functools

import jax
import jax.numpy as jnp
from jax import lax
from jax.experimental import pallas as pl
from jax.experimental.pallas import tpu as pltpu
from jax.sharding import PartitionSpec as P

CAP = 2
RIDGE_TERM = 0.002
NT = (((1,), (1,)), ((), ()))
VMEM = pltpu.VMEM
ANY = pl.ANY


def outgoing_tiles(requests, sender_visit, tile_count):
    is_sender = (requests == sender_visit).astype(jnp.int32)
    before = jnp.cumsum(is_sender, axis=1) - is_sender
    tile_ids = jnp.arange(2 * tile_count, dtype=jnp.int32)[None, :] // 2
    picked = [
        jnp.sum(jnp.where((is_sender == 1) & (before == slot), tile_ids, 0), axis=1)
        for slot in range(CAP)
    ]
    return jnp.stack(picked, axis=1).reshape(-1)


def arrival_slots(sources):
    count = sources.shape[0]
    same_source = sources[:, None] == sources[None, :]
    earlier = jnp.arange(count)[None, :] < jnp.arange(count)[:, None]
    return sources * CAP + jnp.sum((same_source & earlier).astype(jnp.int32), axis=1)


def send_pack_kernel(index_ref, tiles_ref, out_ref, sems):
    slots = out_ref.shape[0]

    def copy(slot):
        return pltpu.make_async_copy(
            tiles_ref.at[index_ref[slot]], out_ref.at[slot], sems.at[slot]
        )

    for slot in range(slots):
        copy(slot).start()
    for slot in range(slots):
        copy(slot).wait()


def send_pack(indices, tiles):
    slots = indices.shape[0]
    return pl.pallas_call(
        send_pack_kernel,
        out_shape=jax.ShapeDtypeStruct((slots,) + tiles.shape[1:], tiles.dtype),
        grid_spec=pltpu.PrefetchScalarGridSpec(
            num_scalar_prefetch=1,
            grid=(1,),
            in_specs=[pl.BlockSpec(tiles.shape, lambda i, s: (0, 0, 0))],
            out_specs=pl.BlockSpec(memory_space=ANY),
            scratch_shapes=[pltpu.SemaphoreType.DMA((slots,))],
        ),
    )(indices, tiles)


def group_pack_kernel(index_ref, arrived_ref, tiles_ref, out_ref, sems):
    owners, per_owner = out_ref.shape[0], out_ref.shape[1]
    science = tiles_ref.shape[0] // owners
    systems = per_owner - science
    copies = []
    for owner in range(owners):
        for place in range(systems):
            copies.append((arrived_ref.at[index_ref[owner * systems + place]], owner, place))
        for place in range(science):
            copies.append((tiles_ref.at[owner * science + place], owner, systems + place))
    started = []
    for number, (source, owner, place) in enumerate(copies):
        copy = pltpu.make_async_copy(source, out_ref.at[owner, place], sems.at[number])
        copy.start()
        started.append(copy)
    for copy in started:
        copy.wait()


def group_pack(indices, arrived, tiles, owners):
    tile_count = tiles.shape[0]
    per_owner = 3 * tile_count // owners
    shape = (owners, per_owner) + tiles.shape[1:]
    return pl.pallas_call(
        group_pack_kernel,
        out_shape=jax.ShapeDtypeStruct(shape, tiles.dtype),
        grid_spec=pltpu.PrefetchScalarGridSpec(
            num_scalar_prefetch=1,
            grid=(1,),
            in_specs=[pl.BlockSpec(memory_space=ANY), pl.BlockSpec(memory_space=ANY)],
            out_specs=pl.BlockSpec(shape, lambda i, s: (0, 0, 0, 0)),
            scratch_shapes=[pltpu.SemaphoreType.DMA((3 * tile_count,))],
        ),
    )(indices, arrived, tiles)


def tables_kernel(half_width, x_ref, y_ref, xtab_ref, ytab_ref):
    taps = x_ref.shape[1]
    step = pl.program_id(0)
    height = 128

    def toeplitz(ref, kernel, offsets):
        total = jnp.zeros(offsets.shape, jnp.float32)
        for tap in range(taps):
            total = jnp.where(offsets == tap, ref[kernel, tap], total)
        return total.astype(jnp.bfloat16)

    r = lax.broadcasted_iota(jnp.int32, (height, 128), 0)
    l = lax.broadcasted_iota(jnp.int32, (height, 128), 1)
    for place in range(2):
        kernel = 2 * step + place
        rows = slice(place * 128, place * 128 + 128)
        xtab_ref[0, rows] = toeplitz(x_ref, kernel, l - r)
        xtab_ref[1, rows] = toeplitz(x_ref, kernel, l + 128 - r)
        ytab_ref[0, place, rows] = toeplitz(y_ref, kernel, r - l + half_width)
        ytab_ref[0, 1 - place, rows] = jnp.zeros((128, 128), jnp.bfloat16)


def filter_tables(x_filters, row_filters, half_width):
    kernel_total, taps = x_filters.shape
    pairs = kernel_total // 2
    smem = pl.BlockSpec(memory_space=pltpu.SMEM)
    return pl.pallas_call(
        functools.partial(tables_kernel, half_width),
        out_shape=(
            jax.ShapeDtypeStruct((2, kernel_total * 128, 128), jnp.bfloat16),
            jax.ShapeDtypeStruct((pairs, 2, 256, 128), jnp.bfloat16),
        ),
        grid=(pairs,),
        in_specs=[smem, smem],
        out_specs=(
            pl.BlockSpec((2, 256, 128), lambda i: (0, i, 0)),
            pl.BlockSpec((1, 2, 256, 128), lambda i: (i, 0, 0, 0)),
        ),
        cost_estimate=pl.CostEstimate(flops=pairs * 21 * 400000, bytes_accessed=5 * 1024 * 1024, transcendentals=0),
    )(x_filters.astype(jnp.float32), row_filters.astype(jnp.float32))


def lane_tiles(ref, row_count):
    tiles = []
    for across in range(2):
        for tile in range(ref.shape[3] // 128):
            lanes = slice(tile * 128, tile * 128 + 128)
            tiles.append(jnp.concatenate([ref[2 * across, 0, :, lanes], ref[2 * across + 1, 0, :, lanes]], axis=0))
    return tiles


def normals_kernel(
    half_width, chunk, bounds_ref, template_ref, science_ref, xtab_ref, ytab_ref, out_ref,
    window, science, smooth, stack, mask, first, second, third,
):
    system = pl.program_id(0)
    row_start, col_start = bounds_ref[2 * system], bounds_ref[2 * system + 1]
    rows = 128
    pairs = ytab_ref.shape[0]
    kernel_total = 2 * pairs
    span = 2 * rows
    groups = span // 16
    tiles = lane_tiles(template_ref, rows)
    count = len(tiles)
    lane = lax.broadcasted_iota(jnp.int32, (rows, 128), 1)
    rolled = [pltpu.roll(tile.astype(jnp.float32), half_width, axis=1) for tile in tiles]
    zero = jnp.zeros((rows, 128), jnp.float32)
    for place in range(count + 1):
        before = rolled[place - 1] if place > 0 else zero
        here = rolled[place] if place < count else zero
        window[place] = jnp.where(lane < half_width, before, here).astype(jnp.bfloat16)
    for place, tile in enumerate(lane_tiles(science_ref, rows)):
        science[place] = tile
    first[...] = jnp.zeros_like(first)
    second[...] = jnp.zeros_like(second)
    third[...] = jnp.zeros_like(third)
    low, high, tall = 256, 512, 16 * (kernel_total + 1)

    def put(start, values):
        for group in range(groups):
            stack[group, pl.ds(start, 16), :] = values[group * 16 : group * 16 + 16]

    def part_body(part, carry):
        c = lax.broadcasted_iota(jnp.int32, (span, rows), 0) + part * span
        a = lax.broadcasted_iota(jnp.int32, (span, rows), 1)
        mask[...] = ((c >= col_start) & (a >= row_start)).astype(jnp.bfloat16)
        ones = (
            lax.broadcasted_iota(jnp.int32, (span, span), 0)
            == lax.broadcasted_iota(jnp.int32, (span, span), 1)
        ).astype(jnp.bfloat16)
        own = jnp.concatenate([science[2 * part], science[2 * part + 1]], axis=1)
        own = lax.dot_general(ones, own, NT, preferred_element_type=jnp.float32)
        put(kernel_total * 16, own.astype(jnp.bfloat16) * mask[...])

        left, middle, right = window[2 * part], window[2 * part + 1], window[2 * part + 2]
        data = jnp.concatenate(
            [jnp.concatenate([left, middle], axis=1), jnp.concatenate([middle, right], axis=1)], axis=0
        )

        def smooth_chunk(number):
            height = chunk * span
            base = number * height
            lhs = jnp.concatenate(
                [xtab_ref[0, pl.ds(base, height), :], xtab_ref[1, pl.ds(base, height), :]], axis=1
            )
            out = lax.dot_general(lhs, data, NT, preferred_element_type=jnp.float32).astype(jnp.bfloat16)
            slot = number % 2
            smooth[slot, 0] = out[:, :rows]
            smooth[slot, 1] = out[:, rows:]

        def basis_chunk(number):
            slot = number % 2
            for place in range(chunk):
                pair = number * chunk + place
                k1, k2 = slice(place * span, place * span + rows), slice(place * span + rows, place * span + span)
                lhs = jnp.concatenate(
                    [
                        jnp.concatenate([smooth[slot, 0, k1], smooth[slot, 0, k2]], axis=1),
                        jnp.concatenate([smooth[slot, 1, k1], smooth[slot, 1, k2]], axis=1),
                    ],
                    axis=0,
                )
                table = jnp.concatenate([ytab_ref[pair, 0], ytab_ref[pair, 1]], axis=1)
                basis = jnp.dot(lhs, table, preferred_element_type=jnp.float32).astype(jnp.bfloat16)
                base = pair * 32 if isinstance(pair, int) else pl.multiple_of(pair * 32, 32)
                put(base, basis[:, :rows] * mask[...])
                put(base + 16, basis[:, rows:] * mask[...])

        steps = pairs // chunk
        smooth_chunk(0)
        for number in range(steps):
            if number + 1 < steps:
                smooth_chunk(number + 1)
            basis_chunk(number)

        def operand(start, stop):
            return jnp.concatenate([stack[group, start:stop, :] for group in range(groups)], axis=1)

        def gram(lhs, rhs):
            return lax.dot_general(lhs, rhs, NT, preferred_element_type=jnp.float32)

        x0, x1, x2 = operand(0, low), operand(low, high), operand(high, tall)
        first[:low] += gram(x0, x0)
        first[low:] += gram(x2, x0)
        second[:low] += gram(x0, x1)
        second[low:high] += gram(x1, x1)
        second[high:] += gram(x2, x1)
        third[...] += gram(x2, x2)
        return carry

    lax.fori_loop(col_start // span, count * 128 // span, part_body, 0)

    def fold(ref):
        height, width = ref.shape
        r = lax.broadcasted_iota(jnp.int32, (height, width), 0)
        l = lax.broadcasted_iota(jnp.int32, (height, width), 1)
        kept = jnp.where((r % 16) == (l % 16), ref[...], 0.0)
        summed = jnp.sum(kept.reshape(height // 16, 16, width), axis=1)
        s = lax.broadcasted_iota(jnp.int32, (width, 128), 0)
        t = lax.broadcasted_iota(jnp.int32, (width, 128), 1)
        return jnp.dot(
            summed, ((s // 16) == t).astype(jnp.float32),
            preferred_element_type=jnp.float32, precision=lax.Precision.HIGHEST,
        )

    out_ref[0, 0:25] = fold(first)
    out_ref[0, 32:73] = fold(second)
    out_ref[0, 80:89] = fold(third)


CHUNK = 4


def normals(bounds, gathered, xtab, ytab, half_width):
    owners, per_owner, half_rows, half_cols = gathered.shape
    systems = 2 * per_owner // 3
    rows, cols = 2 * half_rows, 2 * half_cols
    span = 2 * rows
    quarter = (owners, 1, half_rows, half_cols)
    kernel_total = 2 * ytab.shape[0]
    tall = 16 * (kernel_total + 1)
    return pl.pallas_call(
        functools.partial(normals_kernel, half_width, CHUNK),
        out_shape=jax.ShapeDtypeStruct((systems, 96, 128), jnp.float32),
        grid_spec=pltpu.PrefetchScalarGridSpec(
            num_scalar_prefetch=1,
            grid=(systems,),
            in_specs=[
                pl.BlockSpec(quarter, lambda i, s: (0, i, 0, 0)),
                pl.BlockSpec(quarter, lambda i, s: (0, systems + i // 2, 0, 0)),
                pl.BlockSpec(xtab.shape, lambda i, s: (0, 0, 0)),
                pl.BlockSpec(ytab.shape, lambda i, s: (0, 0, 0, 0)),
            ],
            out_specs=pl.BlockSpec((1, 96, 128), lambda i, s: (i, 0, 0)),
            scratch_shapes=[
                VMEM((cols // 128 + 1, rows, 128), jnp.bfloat16),
                VMEM((cols // 128, rows, 128), jnp.bfloat16),
                VMEM((2, 2, CHUNK * span, rows), jnp.bfloat16),
                VMEM((span // 16, tall, rows), jnp.bfloat16),
                VMEM((span, rows), jnp.bfloat16),
                VMEM((256 + tall - 512, 256), jnp.float32),
                VMEM((tall, 256), jnp.float32),
                VMEM((tall - 512, tall - 512), jnp.float32),
            ],
        ),
        compiler_params=pltpu.CompilerParams(vmem_limit_bytes=56 * 1024 * 1024),
    )(bounds, gathered, gathered, xtab, ytab)


def solve_kernel(kernel_total, pixel_values, blocks_ref, out_ref):
    systems = blocks_ref.shape[0]
    r = lax.broadcasted_iota(jnp.int32, (128, 128), 0)
    l = lax.broadcasted_iota(jnp.int32, (128, 128), 1)
    matrices = []
    for system in range(systems):
        blocks = blocks_ref[system]
        first, second, third = blocks[0:32], blocks[32:80], blocks[80:96]
        zero = jnp.zeros((16, 128), jnp.float32)
        left = jnp.concatenate([first[:16], zero, first[16:32]] + [zero] * 5, axis=0)
        middle = jnp.concatenate([pltpu.roll(second, 16, axis=1)] + [zero] * 5, axis=0)
        right = jnp.concatenate([zero, zero, pltpu.roll(third, 32, axis=1)] + [zero] * 5, axis=0)
        left = jnp.where((l < 16) & ((r < 16) | ((r >= 32) & (r <= kernel_total))), left, 0.0)
        middle = jnp.where((l >= 16) & (l < 32) & (r <= kernel_total), middle, 0.0)
        right = jnp.where((l >= 32) & (l <= kernel_total) & (r >= 32) & (r <= kernel_total), right, 0.0)
        known = left + middle + right
        other = jnp.transpose(known)
        absent = ((r >= 16) & (r < 32) & (l < 16)) | ((l >= 32) & (r < 32))
        whole = jnp.where(absent, other, known) / pixel_values
        whole = whole + jnp.where((r == l) & (r < kernel_total), RIDGE_TERM, 0.0)
        matrices.append(whole[:kernel_total])
    work = jnp.stack(matrices, axis=0)
    row_ids = lax.broadcasted_iota(jnp.int32, (1, kernel_total, 1), 1)
    for pivot in range(kernel_total):
        row = work[:, pivot : pivot + 1, :]
        row = row / row[:, :, pivot : pivot + 1]
        column = work[:, :, pivot : pivot + 1]
        work = jnp.where(row_ids == pivot, row, work - column * row)
    lanes = lax.broadcasted_iota(jnp.int32, work.shape, 2)
    out_ref[...] = jnp.sum(jnp.where(lanes == kernel_total, work, 0.0), axis=2)


def solve(blocks, kernel_total, pixel_values):
    return pl.pallas_call(
        functools.partial(solve_kernel, kernel_total, float(pixel_values)),
        out_shape=jax.ShapeDtypeStruct((blocks.shape[0], kernel_total), jnp.float32),
    )(blocks)


def body(images, partners, coverage, x_filters, row_filters):
    visit = lax.axis_index("visit")
    own_tiles = images[0]
    tile_count, row_count, col_count = own_tiles.shape
    half_width = (x_filters.shape[1] - 1) // 2
    kernel_total = x_filters.shape[0]
    visit_count = partners.shape[0]
    owners = lax.axis_size("tx") * lax.axis_size("ty")
    requests = partners.reshape(visit_count, 2 * tile_count)
    own_requests = lax.dynamic_index_in_dim(requests, visit, 0, keepdims=False)
    sent = send_pack(outgoing_tiles(requests, visit, tile_count), own_tiles)
    arrived = lax.all_to_all(
        sent.reshape((visit_count, CAP) + own_tiles.shape[1:]), "visit", split_axis=0, concat_axis=0, tiled=True
    )
    arrived = arrived.reshape((visit_count * CAP,) + own_tiles.shape[1:])
    grouped = group_pack(arrival_slots(own_requests), arrived, own_tiles, owners)
    gathered = lax.all_to_all(grouped, ("tx", "ty"), split_axis=0, concat_axis=0, tiled=True)

    blocks = coverage[0]
    block_size = row_count // blocks.shape[2]
    row_blocks = jnp.max(blocks, axis=3).sum(axis=2)
    col_blocks = jnp.max(blocks, axis=2).sum(axis=2)
    counts = jnp.stack([row_blocks, col_blocks], axis=-1).astype(jnp.float32)
    counts = lax.all_to_all(
        counts.reshape(owners, 2 * tile_count // owners, 2), ("tx", "ty"), split_axis=0, concat_axis=0, tiled=True
    )
    row_start = 2 * row_count - block_size * (counts[2, :, 0] + counts[3, :, 0])
    col_start = 2 * col_count - block_size * (counts[1, :, 1] + counts[3, :, 1])
    bounds = jnp.stack([row_start, col_start], axis=-1).astype(jnp.int32).reshape(-1)

    xtab, ytab = filter_tables(x_filters, row_filters, half_width)
    sums = normals(bounds, gathered, xtab, ytab, half_width)
    pixel_values = row_count * col_count * owners
    coefficients = solve(sums, kernel_total, pixel_values)
    return coefficients.reshape(1, tile_count // owners, 2, kernel_total)


def solution(mesh):
    return jax.shard_map(
        body,
        mesh=mesh,
        in_specs=(P("visit", None, "ty", "tx"), P(), P("visit", None, None, "ty", "tx"), P(), P()),
        out_specs=P("visit", ("tx", "ty"), None, None),
        check_vma=False,
    )
```

```python
import functools

import jax
import jax.numpy as jnp
from jax import lax
from jax.experimental import pallas as pl
from jax.experimental.pallas import tpu as pltpu
from jax.sharding import PartitionSpec as P

CAP = 2
RIDGE_TERM = 0.002
NT = (((1,), (1,)), ((), ()))
VMEM = pltpu.VMEM
ANY = pl.ANY


def outgoing_tiles(requests, sender_visit, tile_count):
    is_sender = (requests == sender_visit).astype(jnp.int32)
    before = jnp.cumsum(is_sender, axis=1) - is_sender
    tile_ids = jnp.arange(2 * tile_count, dtype=jnp.int32)[None, :] // 2
    picked = [
        jnp.sum(jnp.where((is_sender == 1) & (before == slot), tile_ids, 0), axis=1)
        for slot in range(CAP)
    ]
    return jnp.stack(picked, axis=1).reshape(-1)


def arrival_slots(sources):
    count = sources.shape[0]
    same_source = sources[:, None] == sources[None, :]
    earlier = jnp.arange(count)[None, :] < jnp.arange(count)[:, None]
    return sources * CAP + jnp.sum((same_source & earlier).astype(jnp.int32), axis=1)


MESH = pl.DeviceIdType.MESH
GROUP = ((0, 1), (1, 1), (1, 0))


def exchange_kernel(
    send_ref, slot_ref, tiles, counts, out, counts_out, send_a, recv_a, send_b,
    sent_a, got_a, sent_b, got_b, sent_c, got_c, sent_d, got_d, local,
):
    visits = lax.axis_size("visit")
    visit, tx, ty = lax.axis_index("visit"), lax.axis_index("tx"), lax.axis_index("ty")
    own = tx * 2 + ty
    owners, systems = out.shape[0], slot_ref.shape[0] // out.shape[0]
    share = tiles.shape[0] // owners

    def pack(place, carry):
        for slot in range(CAP):
            send_a[place, slot] = tiles[send_ref[CAP * place + slot]]
        return carry

    lax.fori_loop(0, visits, pack, 0)

    barrier = pltpu.get_barrier_semaphore()
    for step in range(1, visits):
        pl.semaphore_signal(barrier, inc=1, device_id=((visit + step) % visits, tx, ty), device_id_type=MESH)
    for dx, dy in GROUP:
        pl.semaphore_signal(barrier, inc=1, device_id=(visit, (tx + dx) % 2, (ty + dy) % 2), device_id_type=MESH)
    pl.semaphore_wait(barrier, visits - 1 + len(GROUP))

    copies_a = []
    for step in range(1, visits):
        target = (visit + step) % visits
        copies_a.append(
            pltpu.make_async_remote_copy(
                send_a.at[target], recv_a.at[pl.ds(visit * CAP, CAP)], sent_a.at[step], got_a.at[step],
                device_id=(target, tx, ty), device_id_type=MESH,
            )
        )
    copies_b, copies_c = [], []
    for number, (dx, dy) in enumerate(GROUP):
        px, py = (tx + dx) % 2, (ty + dy) % 2
        peer = px * 2 + py
        place = dict(device_id=(visit, px, py), device_id_type=MESH)
        copies_c.append(
            pltpu.make_async_remote_copy(
                tiles.at[pl.ds(share * peer, share)], out.at[own, pl.ds(systems, share)],
                sent_c.at[number], got_c.at[number], **place,
            )
        )
        copies_c.append(
            pltpu.make_async_remote_copy(
                counts.at[peer], counts_out.at[own], sent_d.at[number], got_d.at[number], **place,
            )
        )
        copies_b.append(
            pltpu.make_async_remote_copy(
                send_b.at[peer], out.at[own, pl.ds(0, systems)], sent_b.at[number], got_b.at[number], **place,
            )
        )
    keep = pltpu.make_async_copy(send_a.at[visit], recv_a.at[pl.ds(visit * CAP, CAP)], local.at[0])
    science = pltpu.make_async_copy(
        tiles.at[pl.ds(share * own, share)], out.at[own, pl.ds(systems, share)], local.at[1]
    )
    tally = pltpu.make_async_copy(counts.at[own], counts_out.at[own], local.at[2])
    last = pltpu.make_async_copy(send_b.at[own], out.at[own, pl.ds(0, systems)], local.at[3])
    for copy in copies_a:
        copy.start()
    keep.start()
    for copy in copies_c:
        copy.start()
    science.start()
    tally.start()
    keep.wait()
    for copy in copies_a:
        copy.wait_recv()
    for number, (dx, dy) in enumerate(GROUP):
        peer = ((tx + dx) % 2) * 2 + (ty + dy) % 2
        for place in range(systems):
            send_b[peer, place] = recv_a[slot_ref[peer * systems + place]]
        copies_b[number].start()
    for place in range(systems):
        send_b[own, place] = recv_a[slot_ref[own * systems + place]]
    last.start()
    for copy in copies_b:
        copy.wait()
    for copy in copies_c:
        copy.wait()
    for copy in copies_a:
        copy.wait_send()
    science.wait()
    tally.wait()
    last.wait()


def exchange(send_index, slot_index, tiles, counts):
    owners = counts.shape[0]
    tile_count = tiles.shape[0]
    tile = tiles.shape[1:]
    slots = send_index.shape[0]
    systems = 2 * tile_count // owners
    smem, vmem = pl.BlockSpec(memory_space=pltpu.SMEM), pl.BlockSpec(memory_space=VMEM)
    dma = pltpu.SemaphoreType.DMA
    peers = len(GROUP)
    return pl.pallas_call(
        exchange_kernel,
        out_shape=(
            jax.ShapeDtypeStruct((owners, 3 * tile_count // owners) + tile, tiles.dtype),
            jax.ShapeDtypeStruct(counts.shape, counts.dtype),
        ),
        in_specs=[smem, smem, vmem, vmem],
        out_specs=(pl.BlockSpec(memory_space=ANY), vmem),
        scratch_shapes=[
            VMEM((slots // CAP, CAP) + tile, tiles.dtype),
            VMEM((slots,) + tile, tiles.dtype),
            VMEM((owners, systems) + tile, tiles.dtype),
            dma((slots // CAP,)), dma((slots // CAP,)),
            dma((peers,)), dma((peers,)), dma((peers,)), dma((peers,)), dma((peers,)), dma((peers,)),
            dma((4,)),
        ],
        compiler_params=pltpu.CompilerParams(collective_id=0, has_side_effects=True),
    )(send_index, slot_index, tiles, counts)


def tables_kernel(half_width, x_ref, y_ref, xtab_ref, ytab_ref):
    height = 128
    r = lax.broadcasted_iota(jnp.int32, (height, 128), 0)
    l = lax.broadcasted_iota(jnp.int32, (height, 128), 1)
    near = jnp.abs(r - l) <= half_width

    def shifted(row):
        return pltpu.roll(jnp.broadcast_to(row, (height, row.shape[1])), 0, axis=1, stride=1, stride_axis=0)

    def body(pair, carry):
        for place in range(2):
            kernel = 2 * pair + place
            rows = pl.ds(pl.multiple_of(kernel * height, height), height)
            table = shifted(x_ref[pl.ds(kernel, 1), :]).astype(jnp.bfloat16)
            xtab_ref[0, rows] = table[:, :128]
            xtab_ref[1, rows] = table[:, 128:]
            table = jnp.where(near, shifted(y_ref[pl.ds(kernel, 1), :]), 0.0).astype(jnp.bfloat16)
            half = slice(place * height, place * height + height)
            ytab_ref[pair, place, half] = table
            ytab_ref[pair, 1 - place, half] = jnp.zeros((height, 128), jnp.bfloat16)
        return carry

    lax.fori_loop(0, ytab_ref.shape[0], body, 0)


def filter_tables(x_filters, row_filters, half_width):
    kernel_total, taps = x_filters.shape
    pairs = kernel_total // 2
    x_rows = jnp.pad(x_filters.astype(jnp.float32), ((0, 0), (0, 256 - taps)))
    y_rows = row_filters[:, ::-1].astype(jnp.float32)
    y_rows = jnp.concatenate(
        [y_rows[:, half_width:], jnp.zeros((kernel_total, 128 - taps), jnp.float32), y_rows[:, :half_width]], axis=1
    )
    return pl.pallas_call(
        functools.partial(tables_kernel, half_width),
        out_shape=(
            jax.ShapeDtypeStruct((2, kernel_total * 128, 128), jnp.bfloat16),
            jax.ShapeDtypeStruct((pairs, 2, 256, 128), jnp.bfloat16),
        ),
    )(x_rows, y_rows)


def lane_tiles(ref, row_count):
    tiles = []
    for across in range(2):
        for tile in range(ref.shape[3] // 128):
            lanes = slice(tile * 128, tile * 128 + 128)
            tiles.append(jnp.concatenate([ref[2 * across, 0, :, lanes], ref[2 * across + 1, 0, :, lanes]], axis=0))
    return tiles


def normals_kernel(
    half_width, chunk, bounds_ref, template_ref, science_ref, xtab_ref, ytab_ref, out_ref,
    window, science, smooth, stack, mask, first, second, third,
):
    system = pl.program_id(0)
    row_start, col_start = bounds_ref[2 * system], bounds_ref[2 * system + 1]
    rows = 128
    pairs = ytab_ref.shape[0]
    kernel_total = 2 * pairs
    span = 2 * rows
    groups = span // 16
    tiles = lane_tiles(template_ref, rows)
    count = len(tiles)
    lane = lax.broadcasted_iota(jnp.int32, (rows, 128), 1)
    rolled = [pltpu.roll(tile.astype(jnp.float32), half_width, axis=1) for tile in tiles]
    zero = jnp.zeros((rows, 128), jnp.float32)
    for place in range(count + 1):
        before = rolled[place - 1] if place > 0 else zero
        here = rolled[place] if place < count else zero
        window[place] = jnp.where(lane < half_width, before, here).astype(jnp.bfloat16)
    for place, tile in enumerate(lane_tiles(science_ref, rows)):
        science[place] = tile
    first[...] = jnp.zeros_like(first)
    second[...] = jnp.zeros_like(second)
    third[...] = jnp.zeros_like(third)
    low, high, tall = 256, 512, 16 * (kernel_total + 1)

    def put(start, values):
        for group in range(groups):
            stack[group, pl.ds(start, 16), :] = values[group * 16 : group * 16 + 16]

    def part_body(part, carry):
        c = lax.broadcasted_iota(jnp.int32, (span, rows), 0) + part * span
        a = lax.broadcasted_iota(jnp.int32, (span, rows), 1)
        mask[...] = ((c >= col_start) & (a >= row_start)).astype(jnp.bfloat16)
        ones = (
            lax.broadcasted_iota(jnp.int32, (span, span), 0)
            == lax.broadcasted_iota(jnp.int32, (span, span), 1)
        ).astype(jnp.bfloat16)
        own = jnp.concatenate([science[2 * part], science[2 * part + 1]], axis=1)
        own = lax.dot_general(ones, own, NT, preferred_element_type=jnp.float32)
        put(kernel_total * 16, own.astype(jnp.bfloat16) * mask[...])

        left, middle, right = window[2 * part], window[2 * part + 1], window[2 * part + 2]
        data = jnp.concatenate(
            [jnp.concatenate([left, middle], axis=1), jnp.concatenate([middle, right], axis=1)], axis=0
        )

        def smooth_chunk(number):
            height = chunk * span
            base = number * height
            lhs = jnp.concatenate(
                [xtab_ref[0, pl.ds(base, height), :], xtab_ref[1, pl.ds(base, height), :]], axis=1
            )
            out = lax.dot_general(lhs, data, NT, preferred_element_type=jnp.float32).astype(jnp.bfloat16)
            slot = number % 2
            smooth[slot, 0] = out[:, :rows]
            smooth[slot, 1] = out[:, rows:]

        def basis_chunk(number):
            slot = number % 2
            for place in range(chunk):
                pair = number * chunk + place
                k1, k2 = slice(place * span, place * span + rows), slice(place * span + rows, place * span + span)
                lhs = jnp.concatenate(
                    [
                        jnp.concatenate([smooth[slot, 0, k1], smooth[slot, 0, k2]], axis=1),
                        jnp.concatenate([smooth[slot, 1, k1], smooth[slot, 1, k2]], axis=1),
                    ],
                    axis=0,
                )
                table = jnp.concatenate([ytab_ref[pair, 0], ytab_ref[pair, 1]], axis=1)
                basis = jnp.dot(lhs, table, preferred_element_type=jnp.float32).astype(jnp.bfloat16)
                base = pair * 32 if isinstance(pair, int) else pl.multiple_of(pair * 32, 32)
                put(base, basis[:, :rows] * mask[...])
                put(base + 16, basis[:, rows:] * mask[...])

        steps = pairs // chunk
        smooth_chunk(0)
        for number in range(steps):
            if number + 1 < steps:
                smooth_chunk(number + 1)
            basis_chunk(number)

        def operand(start, stop):
            return jnp.concatenate([stack[group, start:stop, :] for group in range(groups)], axis=1)

        def gram(lhs, rhs):
            return lax.dot_general(lhs, rhs, NT, preferred_element_type=jnp.float32)

        x0, x1, x2 = operand(0, low), operand(low, high), operand(high, tall)
        first[:low] += gram(x0, x0)
        first[low:] += gram(x2, x0)
        second[:low] += gram(x0, x1)
        second[low:high] += gram(x1, x1)
        second[high:] += gram(x2, x1)
        third[...] += gram(x2, x2)
        return carry

    lax.fori_loop(col_start // span, count * 128 // span, part_body, 0)

    def fold(ref):
        height, width = ref.shape
        r = lax.broadcasted_iota(jnp.int32, (height, width), 0)
        l = lax.broadcasted_iota(jnp.int32, (height, width), 1)
        kept = jnp.where((r % 16) == (l % 16), ref[...], 0.0)
        summed = jnp.sum(kept.reshape(height // 16, 16, width), axis=1)
        s = lax.broadcasted_iota(jnp.int32, (width, 128), 0)
        t = lax.broadcasted_iota(jnp.int32, (width, 128), 1)
        return jnp.dot(
            summed, ((s // 16) == t).astype(jnp.float32),
            preferred_element_type=jnp.float32, precision=lax.Precision.HIGHEST,
        )

    out_ref[0, 0:25] = fold(first)
    out_ref[0, 32:73] = fold(second)
    out_ref[0, 80:89] = fold(third)


CHUNK = 4


def normals(bounds, gathered, xtab, ytab, half_width):
    owners, per_owner, half_rows, half_cols = gathered.shape
    systems = 2 * per_owner // 3
    rows, cols = 2 * half_rows, 2 * half_cols
    span = 2 * rows
    quarter = (owners, 1, half_rows, half_cols)
    kernel_total = 2 * ytab.shape[0]
    tall = 16 * (kernel_total + 1)
    return pl.pallas_call(
        functools.partial(normals_kernel, half_width, CHUNK),
        out_shape=jax.ShapeDtypeStruct((systems, 96, 128), jnp.float32),
        grid_spec=pltpu.PrefetchScalarGridSpec(
            num_scalar_prefetch=1,
            grid=(systems,),
            in_specs=[
                pl.BlockSpec(quarter, lambda i, s: (0, i, 0, 0)),
                pl.BlockSpec(quarter, lambda i, s: (0, systems + i // 2, 0, 0)),
                pl.BlockSpec(xtab.shape, lambda i, s: (0, 0, 0)),
                pl.BlockSpec(ytab.shape, lambda i, s: (0, 0, 0, 0)),
            ],
            out_specs=pl.BlockSpec((1, 96, 128), lambda i, s: (i, 0, 0)),
            scratch_shapes=[
                VMEM((cols // 128 + 1, rows, 128), jnp.bfloat16),
                VMEM((cols // 128, rows, 128), jnp.bfloat16),
                VMEM((2, 2, CHUNK * span, rows), jnp.bfloat16),
                VMEM((span // 16, tall, rows), jnp.bfloat16),
                VMEM((span, rows), jnp.bfloat16),
                VMEM((256 + tall - 512, 256), jnp.float32),
                VMEM((tall, 256), jnp.float32),
                VMEM((tall - 512, tall - 512), jnp.float32),
            ],
        ),
        compiler_params=pltpu.CompilerParams(vmem_limit_bytes=56 * 1024 * 1024),
    )(bounds, gathered, gathered, xtab, ytab)


def solve_kernel(kernel_total, pixel_values, blocks_ref, out_ref):
    systems = blocks_ref.shape[0]
    r = lax.broadcasted_iota(jnp.int32, (128, 128), 0)
    l = lax.broadcasted_iota(jnp.int32, (128, 128), 1)
    matrices = []
    for system in range(systems):
        blocks = blocks_ref[system]
        first, second, third = blocks[0:32], blocks[32:80], blocks[80:96]
        zero = jnp.zeros((16, 128), jnp.float32)
        left = jnp.concatenate([first[:16], zero, first[16:32]] + [zero] * 5, axis=0)
        middle = jnp.concatenate([pltpu.roll(second, 16, axis=1)] + [zero] * 5, axis=0)
        right = jnp.concatenate([zero, zero, pltpu.roll(third, 32, axis=1)] + [zero] * 5, axis=0)
        left = jnp.where((l < 16) & ((r < 16) | ((r >= 32) & (r <= kernel_total))), left, 0.0)
        middle = jnp.where((l >= 16) & (l < 32) & (r <= kernel_total), middle, 0.0)
        right = jnp.where((l >= 32) & (l <= kernel_total) & (r >= 32) & (r <= kernel_total), right, 0.0)
        known = left + middle + right
        other = jnp.transpose(known)
        absent = ((r >= 16) & (r < 32) & (l < 16)) | ((l >= 32) & (r < 32))
        whole = jnp.where(absent, other, known) / pixel_values
        whole = whole + jnp.where((r == l) & (r < kernel_total), RIDGE_TERM, 0.0)
        matrices.append(whole[:kernel_total])
    work = jnp.stack(matrices, axis=0)
    row_ids = lax.broadcasted_iota(jnp.int32, (1, kernel_total, 1), 1)
    for pivot in range(kernel_total):
        row = work[:, pivot : pivot + 1, :]
        row = row / row[:, :, pivot : pivot + 1]
        column = work[:, :, pivot : pivot + 1]
        work = jnp.where(row_ids == pivot, row, work - column * row)
    lanes = lax.broadcasted_iota(jnp.int32, work.shape, 2)
    out_ref[...] = jnp.sum(jnp.where(lanes == kernel_total, work, 0.0), axis=2)


def solve(blocks, kernel_total, pixel_values):
    return pl.pallas_call(
        functools.partial(solve_kernel, kernel_total, float(pixel_values)),
        out_shape=jax.ShapeDtypeStruct((blocks.shape[0], kernel_total), jnp.float32),
    )(blocks)


def body(images, partners, coverage, x_filters, row_filters):
    visit = lax.axis_index("visit")
    own_tiles = images[0]
    tile_count, row_count, col_count = own_tiles.shape
    half_width = (x_filters.shape[1] - 1) // 2
    kernel_total = x_filters.shape[0]
    visit_count = partners.shape[0]
    owners = lax.axis_size("tx") * lax.axis_size("ty")
    requests = partners.reshape(visit_count, 2 * tile_count)
    own_requests = lax.dynamic_index_in_dim(requests, visit, 0, keepdims=False)
    blocks = coverage[0]
    block_size = row_count // blocks.shape[2]
    row_blocks = jnp.max(blocks, axis=3).sum(axis=2)
    col_blocks = jnp.max(blocks, axis=2).sum(axis=2)
    counts = jnp.stack([row_blocks, col_blocks], axis=-1).astype(jnp.float32)
    counts = jnp.pad(counts.reshape(owners, 2 * tile_count // owners, 2), ((0, 0), (0, 0), (0, 126)))
    gathered, counts = exchange(
        outgoing_tiles(requests, visit, tile_count), arrival_slots(own_requests), own_tiles, counts
    )
    row_start = 2 * row_count - block_size * (counts[2, :, 0] + counts[3, :, 0])
    col_start = 2 * col_count - block_size * (counts[1, :, 1] + counts[3, :, 1])
    bounds = jnp.stack([row_start, col_start], axis=-1).astype(jnp.int32).reshape(-1)

    xtab, ytab = filter_tables(x_filters, row_filters, half_width)
    sums = normals(bounds, gathered, xtab, ytab, half_width)
    pixel_values = row_count * col_count * owners
    coefficients = solve(sums, kernel_total, pixel_values)
    return coefficients.reshape(1, tile_count // owners, 2, kernel_total)


def solution(mesh):
    return jax.shard_map(
        body,
        mesh=mesh,
        in_specs=(P("visit", None, "ty", "tx"), P(), P("visit", None, None, "ty", "tx"), P(), P()),
        out_specs=P("visit", ("tx", "ty"), None, None),
        check_vma=False,
    )
```

```python
import functools

import jax
import jax.numpy as jnp
from jax import lax
from jax.experimental import pallas as pl
from jax.experimental.pallas import tpu as pltpu
from jax.sharding import PartitionSpec as P

CAP = 2
RIDGE_TERM = 0.002
NT = (((1,), (1,)), ((), ()))
VMEM = pltpu.VMEM
ANY = pl.ANY


def outgoing_tiles(requests, sender_visit, tile_count):
    is_sender = (requests == sender_visit).astype(jnp.int32)
    before = jnp.cumsum(is_sender, axis=1) - is_sender
    tile_ids = jnp.arange(2 * tile_count, dtype=jnp.int32)[None, :] // 2
    picked = [
        jnp.sum(jnp.where((is_sender == 1) & (before == slot), tile_ids, 0), axis=1)
        for slot in range(CAP)
    ]
    return jnp.stack(picked, axis=1).reshape(-1)


def arrival_slots(sources):
    count = sources.shape[0]
    same_source = sources[:, None] == sources[None, :]
    earlier = jnp.arange(count)[None, :] < jnp.arange(count)[:, None]
    return sources * CAP + jnp.sum((same_source & earlier).astype(jnp.int32), axis=1)


def send_pack_kernel(index_ref, tiles_ref, out_ref, sems):
    slots = out_ref.shape[0]

    def copy(slot):
        return pltpu.make_async_copy(
            tiles_ref.at[index_ref[slot]], out_ref.at[slot], sems.at[slot]
        )

    for slot in range(slots):
        copy(slot).start()
    for slot in range(slots):
        copy(slot).wait()


def send_pack(indices, tiles):
    slots = indices.shape[0]
    return pl.pallas_call(
        send_pack_kernel,
        out_shape=jax.ShapeDtypeStruct((slots,) + tiles.shape[1:], tiles.dtype),
        grid_spec=pltpu.PrefetchScalarGridSpec(
            num_scalar_prefetch=1,
            grid=(1,),
            in_specs=[pl.BlockSpec(tiles.shape, lambda i, s: (0, 0, 0))],
            out_specs=pl.BlockSpec(memory_space=ANY),
            scratch_shapes=[pltpu.SemaphoreType.DMA((slots,))],
        ),
    )(indices, tiles)


def group_pack_kernel(index_ref, arrived_ref, out_ref, sems):
    owners, systems = out_ref.shape[0], out_ref.shape[1]
    started = []
    for owner in range(owners):
        for place in range(systems):
            number = owner * systems + place
            copy = pltpu.make_async_copy(
                arrived_ref.at[index_ref[number]], out_ref.at[owner, place], sems.at[number]
            )
            copy.start()
            started.append(copy)
    for copy in started:
        copy.wait()


def group_pack(indices, arrived, owners):
    count = indices.shape[0]
    shape = (owners, count // owners) + arrived.shape[1:]
    return pl.pallas_call(
        group_pack_kernel,
        out_shape=jax.ShapeDtypeStruct(shape, arrived.dtype),
        grid_spec=pltpu.PrefetchScalarGridSpec(
            num_scalar_prefetch=1,
            grid=(1,),
            in_specs=[pl.BlockSpec(memory_space=VMEM)],
            out_specs=pl.BlockSpec(shape, lambda i, s: (0, 0, 0, 0)),
            scratch_shapes=[pltpu.SemaphoreType.DMA((count,))],
        ),
    )(indices, arrived)


def tables_kernel(half_width, x_ref, y_ref, xtab_ref, ytab_ref):
    height = 128
    r = lax.broadcasted_iota(jnp.int32, (height, 128), 0)
    l = lax.broadcasted_iota(jnp.int32, (height, 128), 1)
    near = jnp.abs(r - l) <= half_width

    def shifted(row):
        return pltpu.roll(jnp.broadcast_to(row, (height, row.shape[1])), 0, axis=1, stride=1, stride_axis=0)

    def body(pair, carry):
        for place in range(2):
            kernel = 2 * pair + place
            rows = pl.ds(pl.multiple_of(kernel * height, height), height)
            table = shifted(x_ref[pl.ds(kernel, 1), :]).astype(jnp.bfloat16)
            xtab_ref[0, rows] = table[:, :128]
            xtab_ref[1, rows] = table[:, 128:]
            table = jnp.where(near, shifted(y_ref[pl.ds(kernel, 1), :]), 0.0).astype(jnp.bfloat16)
            half = slice(place * height, place * height + height)
            ytab_ref[pair, place, half] = table
            ytab_ref[pair, 1 - place, half] = jnp.zeros((height, 128), jnp.bfloat16)
        return carry

    lax.fori_loop(0, ytab_ref.shape[0], body, 0)


def filter_tables(x_filters, row_filters, half_width):
    kernel_total, taps = x_filters.shape
    pairs = kernel_total // 2
    x_rows = jnp.pad(x_filters.astype(jnp.float32), ((0, 0), (0, 256 - taps)))
    y_rows = row_filters[:, ::-1].astype(jnp.float32)
    y_rows = jnp.concatenate(
        [y_rows[:, half_width:], jnp.zeros((kernel_total, 128 - taps), jnp.float32), y_rows[:, :half_width]], axis=1
    )
    return pl.pallas_call(
        functools.partial(tables_kernel, half_width),
        out_shape=(
            jax.ShapeDtypeStruct((2, kernel_total * 128, 128), jnp.bfloat16),
            jax.ShapeDtypeStruct((pairs, 2, 256, 128), jnp.bfloat16),
        ),
    )(x_rows, y_rows)


def lane_tiles(quarter, tile_count):
    tiles = []
    for across in range(2):
        for tile in range(tile_count):
            lanes = slice(tile * 128, tile * 128 + 128)
            tiles.append(jnp.concatenate([quarter(across, 0, lanes), quarter(across, 1, lanes)], axis=0))
    return tiles


def normals_kernel(
    half_width, chunk, bounds_ref, template_ref, near_ref, down_ref, across_ref, far_ref, xtab_ref, ytab_ref,
    out_ref, window, science, smooth, stack, mask, first, second, third,
):
    system = pl.program_id(0)
    row_start, col_start = bounds_ref[2 * system], bounds_ref[2 * system + 1]
    rows = 128
    pairs = ytab_ref.shape[0]
    kernel_total = 2 * pairs
    span = 2 * rows
    groups = span // 16
    half_rows = template_ref.shape[2]
    own_tx, own_ty = bounds_ref[2 * pl.num_programs(0)], bounds_ref[2 * pl.num_programs(0) + 1]

    def template_quarter(tx, ty, lanes):
        return template_ref[2 * tx + ty, system, :, lanes]

    def science_quarter(tx, ty, lanes):
        tile = pl.ds(pl.multiple_of(system * half_rows, half_rows), half_rows)
        same = jnp.where(own_ty == ty, near_ref[tile, lanes], down_ref[tile, lanes])
        other = jnp.where(own_ty == ty, across_ref[tile, lanes], far_ref[tile, lanes])
        return jnp.where(own_tx == tx, same, other)

    tiles = lane_tiles(template_quarter, template_ref.shape[3] // 128)
    count = len(tiles)
    lane = lax.broadcasted_iota(jnp.int32, (rows, 128), 1)
    rolled = [pltpu.roll(tile.astype(jnp.float32), half_width, axis=1) for tile in tiles]
    zero = jnp.zeros((rows, 128), jnp.float32)
    for place in range(count + 1):
        before = rolled[place - 1] if place > 0 else zero
        here = rolled[place] if place < count else zero
        window[place] = jnp.where(lane < half_width, before, here).astype(jnp.bfloat16)
    for place, tile in enumerate(lane_tiles(science_quarter, template_ref.shape[3] // 128)):
        science[place] = tile
    first[...] = jnp.zeros_like(first)
    second[...] = jnp.zeros_like(second)
    third[...] = jnp.zeros_like(third)
    low, high, tall = 256, 512, 16 * (kernel_total + 1)

    def put(start, values):
        for group in range(groups):
            stack[group, pl.ds(start, 16), :] = values[group * 16 : group * 16 + 16]

    def part_body(part, carry):
        c = lax.broadcasted_iota(jnp.int32, (span, rows), 0) + part * span
        a = lax.broadcasted_iota(jnp.int32, (span, rows), 1)
        mask[...] = ((c >= col_start) & (a >= row_start)).astype(jnp.bfloat16)
        ones = (
            lax.broadcasted_iota(jnp.int32, (span, span), 0)
            == lax.broadcasted_iota(jnp.int32, (span, span), 1)
        ).astype(jnp.bfloat16)
        own = jnp.concatenate([science[2 * part], science[2 * part + 1]], axis=1)
        own = lax.dot_general(ones, own, NT, preferred_element_type=jnp.float32)
        put(kernel_total * 16, own.astype(jnp.bfloat16) * mask[...])

        left, middle, right = window[2 * part], window[2 * part + 1], window[2 * part + 2]
        data = jnp.concatenate(
            [jnp.concatenate([left, middle], axis=1), jnp.concatenate([middle, right], axis=1)], axis=0
        )

        def smooth_chunk(number):
            height = chunk * span
            base = number * height
            lhs = jnp.concatenate(
                [xtab_ref[0, pl.ds(base, height), :], xtab_ref[1, pl.ds(base, height), :]], axis=1
            )
            out = lax.dot_general(lhs, data, NT, preferred_element_type=jnp.float32).astype(jnp.bfloat16)
            slot = number % 2
            smooth[slot, 0] = out[:, :rows]
            smooth[slot, 1] = out[:, rows:]

        def basis_chunk(number):
            slot = number % 2
            for place in range(chunk):
                pair = number * chunk + place
                k1, k2 = slice(place * span, place * span + rows), slice(place * span + rows, place * span + span)
                lhs = jnp.concatenate(
                    [
                        jnp.concatenate([smooth[slot, 0, k1], smooth[slot, 0, k2]], axis=1),
                        jnp.concatenate([smooth[slot, 1, k1], smooth[slot, 1, k2]], axis=1),
                    ],
                    axis=0,
                )
                table = jnp.concatenate([ytab_ref[pair, 0], ytab_ref[pair, 1]], axis=1)
                basis = jnp.dot(lhs, table, preferred_element_type=jnp.float32).astype(jnp.bfloat16)
                base = pair * 32 if isinstance(pair, int) else pl.multiple_of(pair * 32, 32)
                put(base, basis[:, :rows] * mask[...])
                put(base + 16, basis[:, rows:] * mask[...])

        steps = pairs // chunk
        smooth_chunk(0)
        for number in range(steps):
            if number + 1 < steps:
                smooth_chunk(number + 1)
            basis_chunk(number)

        def operand(start, stop):
            return jnp.concatenate([stack[group, start:stop, :] for group in range(groups)], axis=1)

        def gram(lhs, rhs):
            return lax.dot_general(lhs, rhs, NT, preferred_element_type=jnp.float32)

        x0, x1, x2 = operand(0, low), operand(low, high), operand(high, tall)
        first[:low] += gram(x0, x0)
        first[low:] += gram(x2, x0)
        second[:low] += gram(x0, x1)
        second[low:high] += gram(x1, x1)
        second[high:] += gram(x2, x1)
        third[...] += gram(x2, x2)
        return carry

    lax.fori_loop(col_start // span, count * 128 // span, part_body, 0)

    def fold(ref):
        height, width = ref.shape
        r = lax.broadcasted_iota(jnp.int32, (height, width), 0)
        l = lax.broadcasted_iota(jnp.int32, (height, width), 1)
        kept = jnp.where((r % 16) == (l % 16), ref[...], 0.0)
        summed = jnp.sum(kept.reshape(height // 16, 16, width), axis=1)
        s = lax.broadcasted_iota(jnp.int32, (width, 128), 0)
        t = lax.broadcasted_iota(jnp.int32, (width, 128), 1)
        return jnp.dot(
            summed, ((s // 16) == t).astype(jnp.float32),
            preferred_element_type=jnp.float32, precision=lax.Precision.HIGHEST,
        )

    out_ref[0, 0:25] = fold(first)
    out_ref[0, 32:73] = fold(second)
    out_ref[0, 80:89] = fold(third)


CHUNK = 4


def normals(bounds, templates, science, xtab, ytab, half_width):
    owners, systems, half_rows, half_cols = templates.shape
    rows, cols = 2 * half_rows, 2 * half_cols
    span = 2 * rows
    kernel_total = 2 * ytab.shape[0]
    tall = 16 * (kernel_total + 1)
    whole = pl.BlockSpec(memory_space=VMEM)
    return pl.pallas_call(
        functools.partial(normals_kernel, half_width, CHUNK),
        out_shape=jax.ShapeDtypeStruct((systems, 96, 128), jnp.float32),
        grid_spec=pltpu.PrefetchScalarGridSpec(
            num_scalar_prefetch=1,
            grid=(systems,),
            in_specs=[
                whole, whole, whole, whole, whole,
                whole, whole,
            ],
            out_specs=pl.BlockSpec((1, 96, 128), lambda i, s: (i, 0, 0)),
            scratch_shapes=[
                VMEM((cols // 128 + 1, rows, 128), jnp.bfloat16),
                VMEM((cols // 128, rows, 128), jnp.bfloat16),
                VMEM((2, 2, CHUNK * span, rows), jnp.bfloat16),
                VMEM((span // 16, tall, rows), jnp.bfloat16),
                VMEM((span, rows), jnp.bfloat16),
                VMEM((256 + tall - 512, 256), jnp.float32),
                VMEM((tall, 256), jnp.float32),
                VMEM((tall - 512, tall - 512), jnp.float32),
            ],
        ),
        cost_estimate=pl.CostEstimate(flops=12_000_000_000, bytes_accessed=8_000_000, transcendentals=0),
        compiler_params=pltpu.CompilerParams(vmem_limit_bytes=56 * 1024 * 1024),
    )(bounds, templates, *science, xtab, ytab)


def solve_kernel(kernel_total, pixel_values, even_ref, odd_ref, out_ref):
    systems = 2 * even_ref.shape[0]
    r = lax.broadcasted_iota(jnp.int32, (128, 128), 0)
    l = lax.broadcasted_iota(jnp.int32, (128, 128), 1)
    matrices = []
    for system in range(systems):
        blocks = (odd_ref if system % 2 else even_ref)[system // 2]
        first, second, third = blocks[0:32], blocks[32:80], blocks[80:96]
        zero = jnp.zeros((16, 128), jnp.float32)
        left = jnp.concatenate([first[:16], zero, first[16:32]] + [zero] * 5, axis=0)
        middle = jnp.concatenate([pltpu.roll(second, 16, axis=1)] + [zero] * 5, axis=0)
        right = jnp.concatenate([zero, zero, pltpu.roll(third, 32, axis=1)] + [zero] * 5, axis=0)
        left = jnp.where((l < 16) & ((r < 16) | ((r >= 32) & (r <= kernel_total))), left, 0.0)
        middle = jnp.where((l >= 16) & (l < 32) & (r <= kernel_total), middle, 0.0)
        right = jnp.where((l >= 32) & (l <= kernel_total) & (r >= 32) & (r <= kernel_total), right, 0.0)
        known = left + middle + right
        other = jnp.transpose(known)
        absent = ((r >= 16) & (r < 32) & (l < 16)) | ((l >= 32) & (r < 32))
        whole = jnp.where(absent, other, known) / pixel_values
        whole = whole + jnp.where((r == l) & (r < kernel_total), RIDGE_TERM, 0.0)
        matrices.append(whole[:kernel_total])
    work = jnp.stack(matrices, axis=0)
    row_ids = lax.broadcasted_iota(jnp.int32, (1, kernel_total, 1), 1)
    for pivot in range(kernel_total):
        row = work[:, pivot : pivot + 1, :]
        row = row / row[:, :, pivot : pivot + 1]
        column = work[:, :, pivot : pivot + 1]
        work = jnp.where(row_ids == pivot, row, work - column * row)
    lanes = lax.broadcasted_iota(jnp.int32, work.shape, 2)
    out_ref[...] = jnp.sum(jnp.where(lanes == kernel_total, work, 0.0), axis=2)


def solve(even, odd, kernel_total, pixel_values):
    return pl.pallas_call(
        functools.partial(solve_kernel, kernel_total, float(pixel_values)),
        out_shape=jax.ShapeDtypeStruct((2 * even.shape[0], kernel_total), jnp.float32),
    )(even, odd)


def body(images, partners, coverage, x_filters, row_filters):
    visit = lax.axis_index("visit")
    own_tiles = images[0]
    tile_count, row_count, col_count = own_tiles.shape
    half_width = (x_filters.shape[1] - 1) // 2
    kernel_total = x_filters.shape[0]
    visit_count = partners.shape[0]
    owners = lax.axis_size("tx") * lax.axis_size("ty")
    requests = partners.reshape(visit_count, 2 * tile_count)
    own_requests = lax.dynamic_index_in_dim(requests, visit, 0, keepdims=False)
    share = tile_count // owners
    group = ("tx", "ty")
    sent = send_pack(outgoing_tiles(requests, visit, tile_count), own_tiles)
    arrived = lax.all_to_all(
        sent.reshape((visit_count, CAP) + own_tiles.shape[1:]), "visit", split_axis=0, concat_axis=0, tiled=True
    )
    arrived = arrived.reshape((visit_count * CAP,) + own_tiles.shape[1:])

    blocks = coverage[0]
    block_size = row_count // blocks.shape[2]
    row_blocks = jnp.max(blocks, axis=3).sum(axis=2)
    col_blocks = jnp.max(blocks, axis=2).sum(axis=2)
    counts = jnp.stack([row_blocks, col_blocks], axis=-1).reshape(owners, 2 * share, 2).astype(own_tiles.dtype)
    counts = jnp.pad(counts, ((0, 0), (0, 16 - 2 * share), (0, col_count - 2)))
    science = jnp.concatenate([own_tiles.reshape(owners, share * row_count, col_count), counts], axis=1)
    tx, ty = lax.axis_index("tx"), lax.axis_index("ty")
    parts, row_blocks, col_blocks = [], 0.0, 0.0
    for dx in range(2):
        for dy in range(2):
            peer_x, peer_y = (tx + dx) % 2, (ty + dy) % 2
            part = lax.dynamic_index_in_dim(science, 2 * peer_x + peer_y, 0, keepdims=False)
            if dx or dy:
                swap = 2 * dx + dy
                part = lax.ppermute(part, group, [(i, i ^ swap) for i in range(owners)])
            parts.append(part)
            tally = part[share * row_count : share * row_count + 2 * share, :2].astype(jnp.float32)
            row_blocks += jnp.where(peer_x == 1, tally[:, 0], 0.0)
            col_blocks += jnp.where(peer_y == 1, tally[:, 1], 0.0)
    row_start = 2 * row_count - block_size * row_blocks
    col_start = 2 * col_count - block_size * col_blocks
    bounds = jnp.stack([row_start, col_start], axis=-1).astype(jnp.int32).reshape(share, 2, 2)
    place = jnp.stack([tx, ty]).astype(jnp.int32)

    xtab, ytab = filter_tables(x_filters, row_filters, half_width)
    slots = arrival_slots(own_requests).reshape(tile_count, 2)
    pixel_values = row_count * col_count * owners
    sums = []
    for partner in range(2):
        templates = lax.all_to_all(
            group_pack(slots[:, partner], arrived, owners), group, split_axis=0, concat_axis=0, tiled=True
        )
        limits = jnp.concatenate([bounds[:, partner].reshape(-1), place])
        sums.append(normals(limits, templates, parts, xtab, ytab, half_width))
    coefficients = solve(*sums, kernel_total, pixel_values)
    return coefficients.reshape(1, tile_count // owners, 2, kernel_total)


def solution(mesh):
    return jax.shard_map(
        body,
        mesh=mesh,
        in_specs=(P("visit", None, "ty", "tx"), P(), P("visit", None, None, "ty", "tx"), P(), P()),
        out_specs=P("visit", ("tx", "ty"), None, None),
        check_vma=False,
    )
```

```python
import functools

import jax
import jax.numpy as jnp
from jax import lax
from jax.experimental import pallas as pl
from jax.experimental.pallas import tpu as pltpu
from jax.sharding import PartitionSpec as P

CAP = 2
RIDGE_TERM = 0.002
NT = (((1,), (1,)), ((), ()))
VMEM = pltpu.VMEM
ANY = pl.ANY
SMALL = pltpu.CompilerParams(vmem_limit_bytes=4 * 1024 * 1024)


def outgoing_tiles(requests, sender_visit, tile_count):
    is_sender = (requests == sender_visit).astype(jnp.int32)
    before = jnp.cumsum(is_sender, axis=1) - is_sender
    tile_ids = jnp.arange(2 * tile_count, dtype=jnp.int32)[None, :] // 2
    picked = [
        jnp.sum(jnp.where((is_sender == 1) & (before == slot), tile_ids, 0), axis=1)
        for slot in range(CAP)
    ]
    return jnp.stack(picked, axis=1).reshape(-1)


def arrival_slots(sources):
    count = sources.shape[0]
    same_source = sources[:, None] == sources[None, :]
    earlier = jnp.arange(count)[None, :] < jnp.arange(count)[:, None]
    return sources * CAP + jnp.sum((same_source & earlier).astype(jnp.int32), axis=1)


def send_pack_kernel(index_ref, tiles_ref, out_ref, sems):
    slots = out_ref.shape[0]

    def copy(slot):
        return pltpu.make_async_copy(
            tiles_ref.at[index_ref[slot]], out_ref.at[slot], sems.at[slot]
        )

    for slot in range(slots):
        copy(slot).start()
    for slot in range(slots):
        copy(slot).wait()


def send_pack(indices, tiles):
    slots = indices.shape[0]
    return pl.pallas_call(
        send_pack_kernel,
        out_shape=jax.ShapeDtypeStruct((slots,) + tiles.shape[1:], tiles.dtype),
        grid_spec=pltpu.PrefetchScalarGridSpec(
            num_scalar_prefetch=1,
            grid=(1,),
            in_specs=[pl.BlockSpec(tiles.shape, lambda i, s: (0, 0, 0))],
            out_specs=pl.BlockSpec(memory_space=pltpu.HBM),
            scratch_shapes=[pltpu.SemaphoreType.DMA((slots,))],
        ),
    )(indices, tiles)


def group_pack_kernel(index_ref, arrived_ref, out_ref, sems):
    owners, systems = out_ref.shape[0], out_ref.shape[1]
    started = []
    for owner in range(owners):
        for place in range(systems):
            number = owner * systems + place
            copy = pltpu.make_async_copy(
                arrived_ref.at[index_ref[number]], out_ref.at[owner, place], sems.at[number]
            )
            copy.start()
            started.append(copy)
    for copy in started:
        copy.wait()


def group_pack(indices, arrived, owners):
    count = indices.shape[0]
    shape = (owners, count // owners) + arrived.shape[1:]
    return pl.pallas_call(
        group_pack_kernel,
        out_shape=jax.ShapeDtypeStruct(shape, arrived.dtype),
        grid_spec=pltpu.PrefetchScalarGridSpec(
            num_scalar_prefetch=1,
            grid=(1,),
            in_specs=[pl.BlockSpec(memory_space=ANY)],
            out_specs=pl.BlockSpec(memory_space=pltpu.HBM),
            scratch_shapes=[pltpu.SemaphoreType.DMA((count,))],
        ),
        compiler_params=SMALL,
    )(indices, arrived)


def tables_kernel(half_width, x_ref, y_ref, xtab_ref, ytab_ref):
    height = 128
    r = lax.broadcasted_iota(jnp.int32, (height, 128), 0)
    l = lax.broadcasted_iota(jnp.int32, (height, 128), 1)
    near = jnp.abs(r - l) <= half_width

    def shifted(row):
        return pltpu.roll(jnp.broadcast_to(row, (height, row.shape[1])), 0, axis=1, stride=1, stride_axis=0)

    def body(pair, carry):
        for place in range(2):
            kernel = 2 * pair + place
            rows = pl.ds(pl.multiple_of(kernel * height, height), height)
            table = shifted(x_ref[pl.ds(kernel, 1), :]).astype(jnp.bfloat16)
            xtab_ref[0, rows] = table[:, :128]
            xtab_ref[1, rows] = table[:, 128:]
            table = jnp.where(near, shifted(y_ref[pl.ds(kernel, 1), :]), 0.0).astype(jnp.bfloat16)
            half = slice(place * height, place * height + height)
            ytab_ref[pair, place, half] = table
            ytab_ref[pair, 1 - place, half] = jnp.zeros((height, 128), jnp.bfloat16)
        return carry

    lax.fori_loop(0, ytab_ref.shape[0], body, 0)


def filter_tables(x_filters, row_filters, half_width):
    kernel_total, taps = x_filters.shape
    pairs = kernel_total // 2
    x_rows = jnp.pad(x_filters.astype(jnp.float32), ((0, 0), (0, 256 - taps)))
    y_rows = row_filters[:, ::-1].astype(jnp.float32)
    y_rows = jnp.concatenate(
        [y_rows[:, half_width:], jnp.zeros((kernel_total, 128 - taps), jnp.float32), y_rows[:, :half_width]], axis=1
    )
    return pl.pallas_call(
        functools.partial(tables_kernel, half_width),
        out_shape=(
            jax.ShapeDtypeStruct((2, kernel_total * 128, 128), jnp.bfloat16),
            jax.ShapeDtypeStruct((pairs, 2, 256, 128), jnp.bfloat16),
        ),
    )(x_rows, y_rows)


def lane_tiles(quarter, tile_count):
    tiles = []
    for across in range(2):
        for tile in range(tile_count):
            lanes = slice(tile * 128, tile * 128 + 128)
            tiles.append(jnp.concatenate([quarter(across, 0, lanes), quarter(across, 1, lanes)], axis=0))
    return tiles


def split_dot(lhs, rhs, left):
    value = lhs if left else rhs
    total = None
    for _ in range(3):
        term = value.astype(jnp.bfloat16)
        value = value - term.astype(jnp.float32)
        part = jnp.dot(*((term, rhs) if left else (lhs, term)), preferred_element_type=jnp.float32)
        total = part if total is None else total + part
    return total


def fold(ref):
    height, width = ref.shape
    count = height // 16
    padded = -(-count // 16) * 16
    values = ref[...].reshape(count, 2, 8, width)
    sub = lax.broadcasted_iota(jnp.int32, (count, 8, width), 1)
    lane = lax.broadcasted_iota(jnp.int32, (count, 8, width), 2) % 16
    kept = jnp.where(lane == sub, values[:, 0], jnp.where(lane == sub + 8, values[:, 1], 0.0))
    kept = kept.reshape(count * 8, width)
    r = lax.broadcasted_iota(jnp.int32, (padded, count * 8), 0)
    l = lax.broadcasted_iota(jnp.int32, (padded, count * 8), 1)
    summed = split_dot((l // 8 == r).astype(jnp.bfloat16), kept, False)
    r = lax.broadcasted_iota(jnp.int32, (width, 128), 0)
    l = lax.broadcasted_iota(jnp.int32, (width, 128), 1)
    return split_dot(summed, (r // 16 == l).astype(jnp.bfloat16), True)


def normals_kernel(
    half_width, chunk, bounds_ref, template_ref, near_ref, down_ref, across_ref, far_ref, xtab_ref, ytab_ref,
    out_ref, window, science, smooth, stack, mask, first, second, third,
):
    system = pl.program_id(0)
    row_start, col_start = bounds_ref[2 * system], bounds_ref[2 * system + 1]
    rows = 128
    pairs = ytab_ref.shape[0]
    kernel_total = 2 * pairs
    span = 2 * rows
    half_rows = template_ref.shape[2]
    own_tx, own_ty = bounds_ref[2 * pl.num_programs(0)], bounds_ref[2 * pl.num_programs(0) + 1]

    def template_quarter(tx, ty, lanes):
        return template_ref[2 * tx + ty, system, :, lanes]

    def science_quarter(tx, ty, lanes):
        tile = pl.ds(pl.multiple_of(system * half_rows, half_rows), half_rows)
        same = jnp.where(own_ty == ty, near_ref[tile, lanes], down_ref[tile, lanes])
        other = jnp.where(own_ty == ty, across_ref[tile, lanes], far_ref[tile, lanes])
        return jnp.where(own_tx == tx, same, other)

    tiles = lane_tiles(template_quarter, template_ref.shape[3] // 128)
    count = len(tiles)
    lane = lax.broadcasted_iota(jnp.int32, (rows, 128), 1)
    rolled = [pltpu.roll(tile.astype(jnp.float32), half_width, axis=1) for tile in tiles]
    zero = jnp.zeros((rows, 128), jnp.float32)
    for place in range(count + 1):
        before = rolled[place - 1] if place > 0 else zero
        here = rolled[place] if place < count else zero
        window[place] = jnp.where(lane < half_width, before, here).astype(jnp.bfloat16)
    for place, tile in enumerate(lane_tiles(science_quarter, template_ref.shape[3] // 128)):
        science[place] = tile
    first[...] = jnp.zeros_like(first)
    second[...] = jnp.zeros_like(second)
    third[...] = jnp.zeros_like(third)
    low, high, tall = 256, 512, 16 * (kernel_total + 1)

    def part_body(block, blocks):
        wide = blocks * rows
        groups = wide // 16
        c = lax.broadcasted_iota(jnp.int32, (wide, rows), 0) + block * rows
        a = lax.broadcasted_iota(jnp.int32, (wide, rows), 1)
        mask[:wide] = ((c >= col_start) & (a >= row_start)).astype(jnp.bfloat16)

        def put(start, values):
            for group in range(groups):
                stack[group, pl.ds(start, 16), :] = values[group * 16 : group * 16 + 16]

        ones = (
            lax.broadcasted_iota(jnp.int32, (wide, wide), 0)
            == lax.broadcasted_iota(jnp.int32, (wide, wide), 1)
        ).astype(jnp.bfloat16)
        own = jnp.concatenate([science[block + i] for i in range(blocks)], axis=1)
        own = lax.dot_general(ones, own, NT, preferred_element_type=jnp.float32)
        put(kernel_total * 16, own.astype(jnp.bfloat16) * mask[:wide])

        data = jnp.concatenate(
            [jnp.concatenate([window[block + i], window[block + i + 1]], axis=1) for i in range(blocks)], axis=0
        )

        def smooth_chunk(number):
            height = chunk * span
            base = number * height
            lhs = jnp.concatenate(
                [xtab_ref[0, pl.ds(base, height), :], xtab_ref[1, pl.ds(base, height), :]], axis=1
            )
            out = lax.dot_general(lhs, data, NT, preferred_element_type=jnp.float32).astype(jnp.bfloat16)
            slot = number % 2
            for i in range(blocks):
                smooth[slot, i] = out[:, i * rows : i * rows + rows]

        def basis_chunk(number):
            slot = number % 2
            for place in range(chunk):
                pair = number * chunk + place
                k1, k2 = slice(place * span, place * span + rows), slice(place * span + rows, place * span + span)
                lhs = jnp.concatenate(
                    [jnp.concatenate([smooth[slot, i, k1], smooth[slot, i, k2]], axis=1) for i in range(blocks)],
                    axis=0,
                )
                table = jnp.concatenate([ytab_ref[pair, 0], ytab_ref[pair, 1]], axis=1)
                basis = jnp.dot(lhs, table, preferred_element_type=jnp.float32).astype(jnp.bfloat16)
                base = pair * 32 if isinstance(pair, int) else pl.multiple_of(pair * 32, 32)
                put(base, basis[:, :rows] * mask[:wide])
                put(base + 16, basis[:, rows:] * mask[:wide])

        steps = pairs // chunk
        smooth_chunk(0)
        for number in range(steps):
            if number + 1 < steps:
                smooth_chunk(number + 1)
            basis_chunk(number)

        def operand(start, stop):
            return jnp.concatenate([stack[group, start:stop, :] for group in range(groups)], axis=1)

        def gram(lhs, rhs):
            return lax.dot_general(lhs, rhs, NT, preferred_element_type=jnp.float32)

        x0, x1, x2 = operand(0, low), operand(low, high), operand(high, tall)
        second[...] += gram(jnp.concatenate([x0, x1, x2], axis=0), x1)
        first[...] += gram(jnp.concatenate([x0, x2], axis=0), x0)
        third[...] += gram(x2, x2)

    first_block = jnp.minimum(col_start // rows, count - 1)

    @pl.when(first_block % 2 == 1)
    def _():
        part_body(first_block, 1)

    def step(part, carry):
        part_body(2 * part, 2)
        return carry

    lax.fori_loop((first_block + 1) // 2, count // 2, step, 0)

    out_ref[0, 0:32] = fold(first)
    out_ref[0, 32:80] = fold(second)
    out_ref[0, 80:96] = fold(third)


CHUNK = 4
VLIM = 28


def normals(bounds, templates, science, xtab, ytab, half_width):
    owners, systems, half_rows, half_cols = templates.shape
    rows, cols = 2 * half_rows, 2 * half_cols
    span = 2 * rows
    kernel_total = 2 * ytab.shape[0]
    tall = 16 * (kernel_total + 1)
    whole = pl.BlockSpec(memory_space=VMEM)
    return pl.pallas_call(
        functools.partial(normals_kernel, half_width, CHUNK),
        out_shape=jax.ShapeDtypeStruct((systems, 96, 128), jnp.float32),
        grid_spec=pltpu.PrefetchScalarGridSpec(
            num_scalar_prefetch=1,
            grid=(systems,),
            in_specs=[
                whole, whole, whole, whole, whole,
                whole, whole,
            ],
            out_specs=pl.BlockSpec((1, 96, 128), lambda i, s: (i, 0, 0)),
            scratch_shapes=[
                VMEM((cols // 128 + 1, rows, 128), jnp.bfloat16),
                VMEM((cols // 128, rows, 128), jnp.bfloat16),
                VMEM((2, 2, CHUNK * span, rows), jnp.bfloat16),
                VMEM((span // 16, tall, rows), jnp.bfloat16),
                VMEM((span, rows), jnp.bfloat16),
                VMEM((256 + tall - 512, 256), jnp.float32),
                VMEM((tall, 256), jnp.float32),
                VMEM((tall - 512, tall - 512), jnp.float32),
            ],
        ),
        cost_estimate=pl.CostEstimate(flops=12_000_000_000, bytes_accessed=8_000_000, transcendentals=0),
        compiler_params=pltpu.CompilerParams(vmem_limit_bytes=VLIM * 1024 * 1024),
    )(bounds, templates, *science, xtab, ytab)


def solve_kernel(kernel_total, pixel_values, even_ref, odd_ref, out_ref):
    systems = 2 * even_ref.shape[0]
    r = lax.broadcasted_iota(jnp.int32, (128, 128), 0)
    l = lax.broadcasted_iota(jnp.int32, (128, 128), 1)
    matrices = []
    for system in range(systems):
        blocks = (odd_ref if system % 2 else even_ref)[system // 2]
        first, second, third = blocks[0:32], blocks[32:80], blocks[80:96]
        zero = jnp.zeros((16, 128), jnp.float32)
        left = jnp.concatenate([first[:16], zero, first[16:32]] + [zero] * 5, axis=0)
        middle = jnp.concatenate([pltpu.roll(second, 16, axis=1)] + [zero] * 5, axis=0)
        right = jnp.concatenate([zero, zero, pltpu.roll(third, 32, axis=1)] + [zero] * 5, axis=0)
        left = jnp.where((l < 16) & ((r < 16) | ((r >= 32) & (r <= kernel_total))), left, 0.0)
        middle = jnp.where((l >= 16) & (l < 32) & (r <= kernel_total), middle, 0.0)
        right = jnp.where((l >= 32) & (l <= kernel_total) & (r >= 32) & (r <= kernel_total), right, 0.0)
        known = left + middle + right
        other = jnp.transpose(known)
        absent = ((r >= 16) & (r < 32) & (l < 16)) | ((l >= 32) & (r < 32))
        whole = jnp.where(absent, other, known) / pixel_values
        whole = whole + jnp.where((r == l) & (r < kernel_total), RIDGE_TERM, 0.0)
        matrices.append(whole[:kernel_total])
    work = jnp.stack(matrices, axis=0)
    row_ids = lax.broadcasted_iota(jnp.int32, (1, kernel_total, 1), 1)
    for pivot in range(kernel_total):
        row = work[:, pivot : pivot + 1, :]
        row = row / row[:, :, pivot : pivot + 1]
        column = work[:, :, pivot : pivot + 1]
        work = jnp.where(row_ids == pivot, row, work - column * row)
    lanes = lax.broadcasted_iota(jnp.int32, work.shape, 2)
    out_ref[...] = jnp.sum(jnp.where(lanes == kernel_total, work, 0.0), axis=2)


def solve(even, odd, kernel_total, pixel_values):
    return pl.pallas_call(
        functools.partial(solve_kernel, kernel_total, float(pixel_values)),
        out_shape=jax.ShapeDtypeStruct((2 * even.shape[0], kernel_total), jnp.float32),
        compiler_params=SMALL,
    )(even, odd)


def body(images, partners, coverage, x_filters, row_filters):
    visit = lax.axis_index("visit")
    own_tiles = images[0]
    tile_count, row_count, col_count = own_tiles.shape
    half_width = (x_filters.shape[1] - 1) // 2
    kernel_total = x_filters.shape[0]
    visit_count = partners.shape[0]
    owners = lax.axis_size("tx") * lax.axis_size("ty")
    requests = partners.reshape(visit_count, 2 * tile_count)
    own_requests = lax.dynamic_index_in_dim(requests, visit, 0, keepdims=False)
    share = tile_count // owners
    group = ("tx", "ty")
    sent = send_pack(outgoing_tiles(requests, visit, tile_count), own_tiles)
    arrived = lax.all_to_all(
        sent.reshape((visit_count, CAP) + own_tiles.shape[1:]), "visit", split_axis=0, concat_axis=0, tiled=True
    )
    arrived = arrived.reshape((visit_count * CAP,) + own_tiles.shape[1:])

    blocks = coverage[0]
    block_size = row_count // blocks.shape[2]
    row_blocks = jnp.max(blocks, axis=3).sum(axis=2)
    col_blocks = jnp.max(blocks, axis=2).sum(axis=2)
    counts = jnp.stack([row_blocks, col_blocks], axis=-1).reshape(owners, 2 * share, 2).astype(own_tiles.dtype)
    counts = jnp.pad(counts, ((0, 0), (0, 16 - 2 * share), (0, col_count - 2)))
    science = jnp.concatenate([own_tiles.reshape(owners, share * row_count, col_count), counts], axis=1)
    tx, ty = lax.axis_index("tx"), lax.axis_index("ty")
    parts, row_blocks, col_blocks = [], 0.0, 0.0
    for dx in range(2):
        for dy in range(2):
            peer_x, peer_y = (tx + dx) % 2, (ty + dy) % 2
            part = lax.dynamic_index_in_dim(science, 2 * peer_x + peer_y, 0, keepdims=False)
            if dx or dy:
                swap = 2 * dx + dy
                part = lax.ppermute(part, group, [(i, i ^ swap) for i in range(owners)])
            parts.append(part)
            tally = part[share * row_count : share * row_count + 2 * share, :2].astype(jnp.float32)
            row_blocks += jnp.where(peer_x == 1, tally[:, 0], 0.0)
            col_blocks += jnp.where(peer_y == 1, tally[:, 1], 0.0)
    row_start = 2 * row_count - block_size * row_blocks
    col_start = 2 * col_count - block_size * col_blocks
    bounds = jnp.stack([row_start, col_start], axis=-1).astype(jnp.int32).reshape(share, 2, 2)
    place = jnp.stack([tx, ty]).astype(jnp.int32)

    xtab, ytab = filter_tables(x_filters, row_filters, half_width)
    slots = arrival_slots(own_requests).reshape(tile_count, 2)
    pixel_values = row_count * col_count * owners
    sums = []
    for partner in range(2):
        templates = lax.all_to_all(
            group_pack(slots[:, partner], arrived, owners), group, split_axis=0, concat_axis=0, tiled=True
        )
        limits = jnp.concatenate([bounds[:, partner].reshape(-1), place])
        sums.append(normals(limits, templates, parts, xtab, ytab, half_width))
    coefficients = solve(*sums, kernel_total, pixel_values)
    return coefficients.reshape(1, tile_count // owners, 2, kernel_total)


def solution(mesh):
    return jax.shard_map(
        body,
        mesh=mesh,
        in_specs=(P("visit", None, "ty", "tx"), P(), P("visit", None, None, "ty", "tx"), P(), P()),
        out_specs=P("visit", ("tx", "ty"), None, None),
        check_vma=False,
    )
```

```python
import functools

import jax
import jax.numpy as jnp
from jax import lax
from jax.experimental import pallas as pl
from jax.experimental.pallas import tpu as pltpu
from jax.sharding import PartitionSpec as P

CAP = 2
RIDGE_TERM = 0.002
NT = (((1,), (1,)), ((), ()))
VMEM = pltpu.VMEM
ANY = pl.ANY
SMALL = pltpu.CompilerParams(vmem_limit_bytes=4 * 1024 * 1024)


def outgoing_tiles(requests, sender_visit, tile_count):
    is_sender = (requests == sender_visit).astype(jnp.int32)
    before = jnp.cumsum(is_sender, axis=1) - is_sender
    tile_ids = jnp.arange(2 * tile_count, dtype=jnp.int32)[None, :] // 2
    picked = [
        jnp.sum(jnp.where((is_sender == 1) & (before == slot), tile_ids, 0), axis=1)
        for slot in range(CAP)
    ]
    return jnp.stack(picked, axis=1).reshape(-1)


def arrival_slots(sources):
    count = sources.shape[0]
    same_source = sources[:, None] == sources[None, :]
    earlier = jnp.arange(count)[None, :] < jnp.arange(count)[:, None]
    return sources * CAP + jnp.sum((same_source & earlier).astype(jnp.int32), axis=1)


def send_pack_kernel(index_ref, tiles_ref, out_ref, sems):
    slots = out_ref.shape[0]

    def copy(slot):
        return pltpu.make_async_copy(
            tiles_ref.at[index_ref[slot]], out_ref.at[slot], sems.at[slot]
        )

    for slot in range(slots):
        copy(slot).start()
    for slot in range(slots):
        copy(slot).wait()


def send_pack(indices, tiles):
    slots = indices.shape[0]
    return pl.pallas_call(
        send_pack_kernel,
        out_shape=jax.ShapeDtypeStruct((slots,) + tiles.shape[1:], tiles.dtype),
        grid_spec=pltpu.PrefetchScalarGridSpec(
            num_scalar_prefetch=1,
            grid=(1,),
            in_specs=[pl.BlockSpec(tiles.shape, lambda i, s: (0, 0, 0))],
            out_specs=pl.BlockSpec(memory_space=pltpu.HBM),
            scratch_shapes=[pltpu.SemaphoreType.DMA((slots,))],
        ),
    )(indices, tiles)


def group_pack_kernel(index_ref, arrived_ref, out_ref, sems):
    owners, systems = out_ref.shape[0], out_ref.shape[1]
    started = []
    for owner in range(owners):
        for place in range(systems):
            number = owner * systems + place
            copy = pltpu.make_async_copy(
                arrived_ref.at[index_ref[number]], out_ref.at[owner, place], sems.at[number]
            )
            copy.start()
            started.append(copy)
    for copy in started:
        copy.wait()


def group_pack(indices, arrived, owners):
    count = indices.shape[0]
    shape = (owners, count // owners) + arrived.shape[1:]
    return pl.pallas_call(
        group_pack_kernel,
        out_shape=jax.ShapeDtypeStruct(shape, arrived.dtype),
        grid_spec=pltpu.PrefetchScalarGridSpec(
            num_scalar_prefetch=1,
            grid=(1,),
            in_specs=[pl.BlockSpec(memory_space=ANY)],
            out_specs=pl.BlockSpec(memory_space=pltpu.HBM),
            scratch_shapes=[pltpu.SemaphoreType.DMA((count,))],
        ),
        compiler_params=SMALL,
    )(indices, arrived)


def tables_kernel(half_width, x_ref, y_ref, xtab_ref, ytab_ref):
    height = 128
    r = lax.broadcasted_iota(jnp.int32, (height, 128), 0)
    l = lax.broadcasted_iota(jnp.int32, (height, 128), 1)
    near = jnp.abs(r - l) <= half_width

    def shifted(row):
        return pltpu.roll(jnp.broadcast_to(row, (height, row.shape[1])), 0, axis=1, stride=1, stride_axis=0)

    def body(pair, carry):
        for place in range(2):
            kernel = 2 * pair + place
            rows = pl.ds(pl.multiple_of(kernel * height, height), height)
            table = shifted(x_ref[pl.ds(kernel, 1), :]).astype(jnp.bfloat16)
            xtab_ref[0, rows] = table[:, :128]
            xtab_ref[1, rows] = table[:, 128:]
            table = jnp.where(near, shifted(y_ref[pl.ds(kernel, 1), :]), 0.0).astype(jnp.bfloat16)
            ytab_ref[rows] = table
        return carry

    lax.fori_loop(0, ytab_ref.shape[0] // (2 * height), body, 0)


def filter_tables(x_filters, row_filters, half_width):
    kernel_total, taps = x_filters.shape
    x_rows = jnp.pad(x_filters.astype(jnp.float32), ((0, 0), (0, 256 - taps)))
    y_rows = row_filters[:, ::-1].astype(jnp.float32)
    y_rows = jnp.concatenate(
        [y_rows[:, half_width:], jnp.zeros((kernel_total, 128 - taps), jnp.float32), y_rows[:, :half_width]], axis=1
    )
    return pl.pallas_call(
        functools.partial(tables_kernel, half_width),
        out_shape=(
            jax.ShapeDtypeStruct((2, kernel_total * 128, 128), jnp.bfloat16),
            jax.ShapeDtypeStruct((kernel_total * 128, 128), jnp.bfloat16),
        ),
        compiler_params=pltpu.CompilerParams(vmem_limit_bytes=12 * 1024 * 1024),
    )(x_rows, y_rows)


def lane_tiles(quarter, tile_count):
    tiles = []
    for across in range(2):
        for tile in range(tile_count):
            lanes = slice(tile * 128, tile * 128 + 128)
            tiles.append(jnp.concatenate([quarter(across, 0, lanes), quarter(across, 1, lanes)], axis=0))
    return tiles


def split_dot(lhs, rhs, left):
    value = lhs if left else rhs
    total = None
    for _ in range(3):
        term = value.astype(jnp.bfloat16)
        value = value - term.astype(jnp.float32)
        part = jnp.dot(*((term, rhs) if left else (lhs, term)), preferred_element_type=jnp.float32)
        total = part if total is None else total + part
    return total


def fold(ref):
    height, width = ref.shape
    count = height // 16
    padded = -(-count // 16) * 16
    values = ref[...].reshape(count, 2, 8, width)
    sub = lax.broadcasted_iota(jnp.int32, (count, 8, width), 1)
    lane = lax.broadcasted_iota(jnp.int32, (count, 8, width), 2) % 16
    kept = jnp.where(lane == sub, values[:, 0], jnp.where(lane == sub + 8, values[:, 1], 0.0))
    kept = kept.reshape(count * 8, width)
    r = lax.broadcasted_iota(jnp.int32, (padded, count * 8), 0)
    l = lax.broadcasted_iota(jnp.int32, (padded, count * 8), 1)
    summed = split_dot((l // 8 == r).astype(jnp.bfloat16), kept, False)
    r = lax.broadcasted_iota(jnp.int32, (width, 128), 0)
    l = lax.broadcasted_iota(jnp.int32, (width, 128), 1)
    return split_dot(summed, (r // 16 == l).astype(jnp.bfloat16), True)


def normals_kernel(
    half_width, chunk, bounds_ref, template_ref, near_ref, down_ref, across_ref, far_ref, xtab_ref, ytab_ref,
    out_ref, window, science, smooth, stack, mask, first, second, third,
):
    system = pl.program_id(0)
    row_start, col_start = bounds_ref[2 * system], bounds_ref[2 * system + 1]
    rows = 128
    pairs = ytab_ref.shape[0] // 256
    kernel_total = 2 * pairs
    span = 2 * rows
    half_rows = template_ref.shape[2]
    own_tx, own_ty = bounds_ref[2 * pl.num_programs(0)], bounds_ref[2 * pl.num_programs(0) + 1]

    def template_quarter(tx, ty, lanes):
        return template_ref[2 * tx + ty, system, :, lanes]

    def science_quarter(tx, ty, lanes):
        tile = pl.ds(pl.multiple_of(system * half_rows, half_rows), half_rows)
        same = jnp.where(own_ty == ty, near_ref[tile, lanes], down_ref[tile, lanes])
        other = jnp.where(own_ty == ty, across_ref[tile, lanes], far_ref[tile, lanes])
        return jnp.where(own_tx == tx, same, other)

    tiles = lane_tiles(template_quarter, template_ref.shape[3] // 128)
    count = len(tiles)
    lane = lax.broadcasted_iota(jnp.int32, (rows, 128), 1)
    rolled = [pltpu.roll(tile.astype(jnp.float32), half_width, axis=1) for tile in tiles]
    zero = jnp.zeros((rows, 128), jnp.float32)
    for place in range(count + 1):
        before = rolled[place - 1] if place > 0 else zero
        here = rolled[place] if place < count else zero
        window[place] = jnp.where(lane < half_width, before, here).astype(jnp.bfloat16)
    for place, tile in enumerate(lane_tiles(science_quarter, template_ref.shape[3] // 128)):
        science[place] = tile

    def clear():
        first[...] = jnp.zeros_like(first)
        second[...] = jnp.zeros_like(second)
        third[...] = jnp.zeros_like(third)

    pl.when(system == 0)(clear)
    low, high, tall = 256, 512, 16 * (kernel_total + 1)

    def part_body(block, blocks):
        wide = blocks * rows
        groups = wide // 16
        c = lax.broadcasted_iota(jnp.int32, (wide, rows), 0) + block * rows
        a = lax.broadcasted_iota(jnp.int32, (wide, rows), 1)
        mask[:wide] = ((c >= col_start) & (a >= row_start)).astype(jnp.bfloat16)

        def put(start, values):
            for group in range(groups):
                stack[group, pl.ds(start, 16), :] = values[group * 16 : group * 16 + 16]

        ones = (
            lax.broadcasted_iota(jnp.int32, (wide, wide), 0)
            == lax.broadcasted_iota(jnp.int32, (wide, wide), 1)
        ).astype(jnp.bfloat16)
        own = jnp.concatenate([science[block + i] for i in range(blocks)], axis=1)
        own = lax.dot_general(ones, own, NT, preferred_element_type=jnp.float32)
        put(kernel_total * 16, own.astype(jnp.bfloat16) * mask[:wide])

        data = jnp.concatenate(
            [jnp.concatenate([window[block + i], window[block + i + 1]], axis=1) for i in range(blocks)], axis=0
        )

        def smooth_chunk(number):
            height = chunk * span
            base = number * height
            lhs = jnp.concatenate(
                [xtab_ref[0, base : base + height, :], xtab_ref[1, base : base + height, :]], axis=1
            )
            out = lax.dot_general(lhs, data, NT, preferred_element_type=jnp.float32).astype(jnp.bfloat16)
            slot = number % 2
            for i in range(blocks):
                smooth[slot, i] = out[:, i * rows : i * rows + rows]

        def basis_chunk(number):
            slot = number % 2
            for place in range(chunk):
                pair = number * chunk + place
                k1, k2 = slice(place * span, place * span + rows), slice(place * span + rows, place * span + span)
                lhs = jnp.concatenate(
                    [jnp.concatenate([smooth[slot, i, k1], smooth[slot, i, k2]], axis=1) for i in range(blocks)],
                    axis=0,
                )
                top = ytab_ref[pair * span : pair * span + rows]
                bottom = ytab_ref[pair * span + rows : pair * span + span]
                blank = jnp.zeros_like(top)
                table = jnp.concatenate(
                    [jnp.concatenate([top, blank], axis=1), jnp.concatenate([blank, bottom], axis=1)], axis=0
                )
                basis = jnp.dot(lhs, table, preferred_element_type=jnp.float32).astype(jnp.bfloat16)
                base = pair * 32 if isinstance(pair, int) else pl.multiple_of(pair * 32, 32)
                put(base, basis[:, :rows] * mask[:wide])
                put(base + 16, basis[:, rows:] * mask[:wide])

        steps = pairs // chunk
        smooth_chunk(0)
        for number in range(steps):
            if number + 1 < steps:
                smooth_chunk(number + 1)
            basis_chunk(number)

        def operand(start, stop):
            return jnp.concatenate([stack[group, start:stop, :] for group in range(groups)], axis=1)

        def gram(lhs, rhs):
            return lax.dot_general(lhs, rhs, NT, preferred_element_type=jnp.float32)

        x0, x1, x2 = operand(0, low), operand(low, high), operand(high, tall)
        second[...] += gram(jnp.concatenate([x0, x1, x2], axis=0), x1)
        first[...] += gram(jnp.concatenate([x0, x2], axis=0), x0)
        third[...] += gram(x2, x2)

    first_block = jnp.minimum(col_start // rows, count - 1)

    @pl.when(first_block % 2 == 1)
    def _():
        part_body(first_block, 1)

    def step(part, carry):
        part_body(2 * part, 2)
        return carry

    lax.fori_loop((first_block + 1) // 2, count // 2, step, 0)

    out_ref[0, 0:32] = fold(first)
    out_ref[0, 32:80] = fold(second)
    out_ref[0, 80:96] = fold(third)
    clear()


CHUNK = 4
VLIM = 24


def normals(bounds, templates, science, tables, half_width):
    owners, systems, half_rows, half_cols = templates.shape
    rows, cols = 2 * half_rows, 2 * half_cols
    span = 2 * rows
    kernel_total = tables[1].shape[0] // 128
    tall = 16 * (kernel_total + 1)
    whole = pl.BlockSpec(memory_space=VMEM)
    return pl.pallas_call(
        functools.partial(normals_kernel, half_width, CHUNK),
        out_shape=jax.ShapeDtypeStruct((systems, 96, 128), jnp.float32),
        grid_spec=pltpu.PrefetchScalarGridSpec(
            num_scalar_prefetch=1,
            grid=(systems,),
            in_specs=[
                whole, whole, whole, whole, whole,
                whole, whole,
            ],
            out_specs=pl.BlockSpec((1, 96, 128), lambda i, s: (i, 0, 0)),
            scratch_shapes=[
                VMEM((cols // 128 + 1, rows, 128), jnp.bfloat16),
                VMEM((cols // 128, rows, 128), jnp.bfloat16),
                VMEM((2, 2, CHUNK * span, rows), jnp.bfloat16),
                VMEM((span // 16, tall, rows), jnp.bfloat16),
                VMEM((span, rows), jnp.bfloat16),
                VMEM((256 + tall - 512, 256), jnp.float32),
                VMEM((tall, 256), jnp.float32),
                VMEM((tall - 512, tall - 512), jnp.float32),
            ],
        ),
        cost_estimate=pl.CostEstimate(flops=12_000_000_000, bytes_accessed=8_000_000, transcendentals=0),
        compiler_params=pltpu.CompilerParams(vmem_limit_bytes=VLIM * 1024 * 1024),
    )(bounds, templates, *science, *tables)


def solve_kernel(kernel_total, pixel_values, even_ref, odd_ref, out_ref):
    systems = 2 * even_ref.shape[0]
    r = lax.broadcasted_iota(jnp.int32, (128, 128), 0)
    l = lax.broadcasted_iota(jnp.int32, (128, 128), 1)
    matrices = []
    for system in range(systems):
        blocks = (odd_ref if system % 2 else even_ref)[system // 2]
        first, second, third = blocks[0:32], blocks[32:80], blocks[80:96]
        zero = jnp.zeros((16, 128), jnp.float32)
        left = jnp.concatenate([first[:16], zero, first[16:32]] + [zero] * 5, axis=0)
        middle = jnp.concatenate([pltpu.roll(second, 16, axis=1)] + [zero] * 5, axis=0)
        right = jnp.concatenate([zero, zero, pltpu.roll(third, 32, axis=1)] + [zero] * 5, axis=0)
        left = jnp.where((l < 16) & ((r < 16) | ((r >= 32) & (r <= kernel_total))), left, 0.0)
        middle = jnp.where((l >= 16) & (l < 32) & (r <= kernel_total), middle, 0.0)
        right = jnp.where((l >= 32) & (l <= kernel_total) & (r >= 32) & (r <= kernel_total), right, 0.0)
        known = left + middle + right
        other = jnp.transpose(known)
        absent = ((r >= 16) & (r < 32) & (l < 16)) | ((l >= 32) & (r < 32))
        whole = jnp.where(absent, other, known) / pixel_values
        whole = whole + jnp.where((r == l) & (r < kernel_total), RIDGE_TERM, 0.0)
        matrices.append(whole[:kernel_total])
    width = kernel_total + 1
    beside = 128 // width
    groups = []
    for start in range(0, systems, beside):
        total = matrices[start]
        for place in range(1, min(beside, systems - start)):
            total = total + pltpu.roll(matrices[start + place], place * width, axis=1)
        groups.append(total)
    row_ids = lax.broadcasted_iota(jnp.int32, (kernel_total, 128), 0)
    base = lax.broadcasted_iota(jnp.int32, (kernel_total, 128), 1) // width * width
    used = lax.broadcasted_iota(jnp.int32, (1, 128), 1) < beside * width
    for pivot in range(kernel_total):
        place = jnp.minimum(base + pivot, 127)
        for number, work in enumerate(groups):
            column = jnp.take_along_axis(work, place, axis=1)
            row = work[pivot : pivot + 1] / jnp.where(used & (base[:1] < (min(beside, systems - number * beside)) * width), column[pivot : pivot + 1], 1.0)
            groups[number] = jnp.where(row_ids == pivot, row, work - column * row)
    for number, work in enumerate(groups):
        turned = jnp.transpose(jnp.concatenate([work, jnp.zeros((128 - kernel_total, 128), jnp.float32)], axis=0))
        for place in range(min(beside, systems - number * beside)):
            last = place * width + kernel_total
            out_ref[number * beside + place : number * beside + place + 1] = turned[last : last + 1, :kernel_total]


def solve(even, odd, kernel_total, pixel_values):
    return pl.pallas_call(
        functools.partial(solve_kernel, kernel_total, float(pixel_values)),
        out_shape=jax.ShapeDtypeStruct((2 * even.shape[0], kernel_total), jnp.float32),
        compiler_params=SMALL,
    )(even, odd)


def body(images, partners, coverage, x_filters, row_filters):
    visit = lax.axis_index("visit")
    own_tiles = images[0]
    tile_count, row_count, col_count = own_tiles.shape
    half_width = (x_filters.shape[1] - 1) // 2
    kernel_total = x_filters.shape[0]
    visit_count = partners.shape[0]
    owners = lax.axis_size("tx") * lax.axis_size("ty")
    requests = partners.reshape(visit_count, 2 * tile_count)
    own_requests = lax.dynamic_index_in_dim(requests, visit, 0, keepdims=False)
    share = tile_count // owners
    group = ("tx", "ty")
    sent = send_pack(outgoing_tiles(requests, visit, tile_count), own_tiles)
    arrived = lax.all_to_all(
        sent.reshape((visit_count, CAP) + own_tiles.shape[1:]), "visit", split_axis=0, concat_axis=0, tiled=True
    )
    arrived = arrived.reshape((visit_count * CAP,) + own_tiles.shape[1:])

    blocks = coverage[0]
    block_size = row_count // blocks.shape[2]
    row_blocks = jnp.max(blocks, axis=3).sum(axis=2)
    col_blocks = jnp.max(blocks, axis=2).sum(axis=2)
    counts = jnp.stack([row_blocks, col_blocks], axis=-1).reshape(owners, 2 * share, 2).astype(own_tiles.dtype)
    counts = jnp.pad(counts, ((0, 0), (0, 16 - 2 * share), (0, col_count - 2)))
    science = jnp.concatenate([own_tiles.reshape(owners, share * row_count, col_count), counts], axis=1)
    tx, ty = lax.axis_index("tx"), lax.axis_index("ty")
    parts, row_blocks, col_blocks = [], 0.0, 0.0
    for dx in range(2):
        for dy in range(2):
            peer_x, peer_y = (tx + dx) % 2, (ty + dy) % 2
            part = lax.dynamic_index_in_dim(science, 2 * peer_x + peer_y, 0, keepdims=False)
            if dx or dy:
                swap = 2 * dx + dy
                part = lax.ppermute(part, group, [(i, i ^ swap) for i in range(owners)])
            parts.append(part)
            tally = part[share * row_count : share * row_count + 2 * share, :2].astype(jnp.float32)
            row_blocks += jnp.where(peer_x == 1, tally[:, 0], 0.0)
            col_blocks += jnp.where(peer_y == 1, tally[:, 1], 0.0)
    row_start = 2 * row_count - block_size * row_blocks
    col_start = 2 * col_count - block_size * col_blocks
    bounds = jnp.stack([row_start, col_start], axis=-1).astype(jnp.int32).reshape(share, 2, 2)
    place = jnp.stack([tx, ty]).astype(jnp.int32)

    slots = arrival_slots(own_requests).reshape(tile_count, 2)
    pixel_values = row_count * col_count * owners
    grouped = [group_pack(slots[:, partner], arrived, owners) for partner in range(2)]
    grouped[0], x_filters, row_filters = lax.optimization_barrier((grouped[0], x_filters, row_filters))
    tables = filter_tables(x_filters, row_filters, half_width)
    sums = []
    for partner in range(2):
        templates = lax.all_to_all(grouped[partner], group, split_axis=0, concat_axis=0, tiled=True)
        limits = jnp.concatenate([bounds[:, partner].reshape(-1), place])
        sums.append(normals(limits, templates, parts, tables, half_width))
    coefficients = solve(*sums, kernel_total, pixel_values)
    return coefficients.reshape(1, tile_count // owners, 2, kernel_total)


def solution(mesh):
    return jax.shard_map(
        body,
        mesh=mesh,
        in_specs=(P("visit", None, "ty", "tx"), P(), P("visit", None, None, "ty", "tx"), P(), P()),
        out_specs=P("visit", ("tx", "ty"), None, None),
        check_vma=False,
    )
```

```python
import functools

import jax
import jax.numpy as jnp
from jax import lax
from jax.experimental import pallas as pl
from jax.experimental.pallas import tpu as pltpu
from jax.sharding import PartitionSpec as P

CAP = 2
RIDGE_TERM = 0.002
NT = (((1,), (1,)), ((), ()))
VMEM = pltpu.VMEM
ANY = pl.ANY
SMALL = pltpu.CompilerParams(vmem_limit_bytes=4 * 1024 * 1024)


def outgoing_tiles(requests, sender_visit, tile_count):
    is_sender = (requests == sender_visit).astype(jnp.int32)
    before = jnp.cumsum(is_sender, axis=1) - is_sender
    tile_ids = jnp.arange(2 * tile_count, dtype=jnp.int32)[None, :] // 2
    picked = [
        jnp.sum(jnp.where((is_sender == 1) & (before == slot), tile_ids, 0), axis=1)
        for slot in range(CAP)
    ]
    return jnp.stack(picked, axis=1).reshape(-1)


def arrival_slots(sources):
    count = sources.shape[0]
    same_source = sources[:, None] == sources[None, :]
    earlier = jnp.arange(count)[None, :] < jnp.arange(count)[:, None]
    return sources * CAP + jnp.sum((same_source & earlier).astype(jnp.int32), axis=1)


def send_pack_kernel(index_ref, tiles_ref, out_ref, sems):
    slots = out_ref.shape[0]

    def copy(slot):
        return pltpu.make_async_copy(
            tiles_ref.at[index_ref[slot]], out_ref.at[slot], sems.at[slot]
        )

    for slot in range(slots):
        copy(slot).start()
    for slot in range(slots):
        copy(slot).wait()


def send_pack(indices, tiles):
    slots = indices.shape[0]
    return pl.pallas_call(
        send_pack_kernel,
        out_shape=jax.ShapeDtypeStruct((slots,) + tiles.shape[1:], tiles.dtype),
        grid_spec=pltpu.PrefetchScalarGridSpec(
            num_scalar_prefetch=1,
            grid=(1,),
            in_specs=[pl.BlockSpec(tiles.shape, lambda i, s: (0, 0, 0))],
            out_specs=pl.BlockSpec(memory_space=pltpu.HBM),
            scratch_shapes=[pltpu.SemaphoreType.DMA((slots,))],
        ),
    )(indices, tiles)


def group_pack_kernel(index_ref, arrived_ref, out_ref, sems):
    owners, systems = out_ref.shape[0], out_ref.shape[1]
    started = []
    for owner in range(owners):
        for place in range(systems):
            number = owner * systems + place
            copy = pltpu.make_async_copy(
                arrived_ref.at[index_ref[number]], out_ref.at[owner, place], sems.at[number]
            )
            copy.start()
            started.append(copy)
    for copy in started:
        copy.wait()


def group_pack(indices, arrived, owners):
    count = indices.shape[0]
    shape = (owners, count // owners) + arrived.shape[1:]
    return pl.pallas_call(
        group_pack_kernel,
        out_shape=jax.ShapeDtypeStruct(shape, arrived.dtype),
        grid_spec=pltpu.PrefetchScalarGridSpec(
            num_scalar_prefetch=1,
            grid=(1,),
            in_specs=[pl.BlockSpec(memory_space=ANY)],
            out_specs=pl.BlockSpec(memory_space=pltpu.HBM),
            scratch_shapes=[pltpu.SemaphoreType.DMA((count,))],
        ),
        compiler_params=SMALL,
    )(indices, arrived)


def tables_kernel(half_width, x_ref, y_ref, xtab_ref, ytab_ref):
    height = 128
    r = lax.broadcasted_iota(jnp.int32, (height, 128), 0)
    l = lax.broadcasted_iota(jnp.int32, (height, 128), 1)
    near = jnp.abs(r - l) <= half_width

    def shifted(row):
        return pltpu.roll(jnp.broadcast_to(row, (height, row.shape[1])), 0, axis=1, stride=1, stride_axis=0)

    def body(pair, carry):
        for place in range(2):
            kernel = 2 * pair + place
            rows = pl.ds(pl.multiple_of(kernel * height, height), height)
            table = shifted(x_ref[pl.ds(kernel, 1), :]).astype(jnp.bfloat16)
            xtab_ref[0, rows] = table[:, :128]
            xtab_ref[1, rows] = table[:, 128:]
            table = jnp.where(near, shifted(y_ref[pl.ds(kernel, 1), :]), 0.0).astype(jnp.bfloat16)
            ytab_ref[rows] = table
        return carry

    lax.fori_loop(0, ytab_ref.shape[0] // (2 * height), body, 0)


def filter_tables(x_filters, row_filters, half_width):
    kernel_total, taps = x_filters.shape
    x_rows = jnp.pad(x_filters.astype(jnp.float32), ((0, 0), (0, 256 - taps)))
    y_rows = row_filters[:, ::-1].astype(jnp.float32)
    y_rows = jnp.concatenate(
        [y_rows[:, half_width:], jnp.zeros((kernel_total, 128 - taps), jnp.float32), y_rows[:, :half_width]], axis=1
    )
    return pl.pallas_call(
        functools.partial(tables_kernel, half_width),
        out_shape=(
            jax.ShapeDtypeStruct((2, kernel_total * 128, 128), jnp.bfloat16),
            jax.ShapeDtypeStruct((kernel_total * 128, 128), jnp.bfloat16),
        ),
    )(x_rows, y_rows)


def lane_tiles(quarter, tile_count):
    tiles = []
    for across in range(2):
        for tile in range(tile_count):
            lanes = slice(tile * 128, tile * 128 + 128)
            tiles.append(jnp.concatenate([quarter(across, 0, lanes), quarter(across, 1, lanes)], axis=0))
    return tiles


def split_dot(lhs, rhs, left):
    value = lhs if left else rhs
    total = None
    for _ in range(3):
        term = value.astype(jnp.bfloat16)
        value = value - term.astype(jnp.float32)
        part = jnp.dot(*((term, rhs) if left else (lhs, term)), preferred_element_type=jnp.float32)
        total = part if total is None else total + part
    return total


def fold(ref):
    height, width = ref.shape
    count = height // 16
    padded = -(-count // 16) * 16
    values = ref[...].reshape(count, 2, 8, width)
    sub = lax.broadcasted_iota(jnp.int32, (count, 8, width), 1)
    lane = lax.broadcasted_iota(jnp.int32, (count, 8, width), 2) % 16
    kept = jnp.where(lane == sub, values[:, 0], jnp.where(lane == sub + 8, values[:, 1], 0.0))
    kept = kept.reshape(count * 8, width)
    r = lax.broadcasted_iota(jnp.int32, (padded, count * 8), 0)
    l = lax.broadcasted_iota(jnp.int32, (padded, count * 8), 1)
    summed = split_dot((l // 8 == r).astype(jnp.bfloat16), kept, False)
    r = lax.broadcasted_iota(jnp.int32, (width, 128), 0)
    l = lax.broadcasted_iota(jnp.int32, (width, 128), 1)
    return split_dot(summed, (r // 16 == l).astype(jnp.bfloat16), True)


def normals_kernel(
    half_width, chunk, bounds_ref, template_ref, near_ref, down_ref, across_ref, far_ref, xtab_ref, ytab_ref,
    out_ref, window, science, smooth, stack, mask, first, second, third,
):
    system = pl.program_id(0)
    row_start, col_start = bounds_ref[2 * system], bounds_ref[2 * system + 1]
    rows = 128
    pairs = ytab_ref.shape[0] // 256
    kernel_total = 2 * pairs
    span = 2 * rows
    half_rows = template_ref.shape[2]
    own_tx, own_ty = bounds_ref[2 * pl.num_programs(0)], bounds_ref[2 * pl.num_programs(0) + 1]

    def template_quarter(tx, ty, lanes):
        return template_ref[2 * tx + ty, system, :, lanes]

    def science_quarter(tx, ty, lanes):
        tile = pl.ds(pl.multiple_of(system * half_rows, half_rows), half_rows)
        same = jnp.where(own_ty == ty, near_ref[tile, lanes], down_ref[tile, lanes])
        other = jnp.where(own_ty == ty, across_ref[tile, lanes], far_ref[tile, lanes])
        return jnp.where(own_tx == tx, same, other)

    tiles = lane_tiles(template_quarter, template_ref.shape[3] // 128)
    count = len(tiles)
    lane = lax.broadcasted_iota(jnp.int32, (rows, 128), 1)
    rolled = [pltpu.roll(tile.astype(jnp.float32), half_width, axis=1) for tile in tiles]
    zero = jnp.zeros((rows, 128), jnp.float32)
    for place in range(count + 1):
        before = rolled[place - 1] if place > 0 else zero
        here = rolled[place] if place < count else zero
        window[place] = jnp.where(lane < half_width, before, here).astype(jnp.bfloat16)
    for place, tile in enumerate(lane_tiles(science_quarter, template_ref.shape[3] // 128)):
        science[place] = tile

    def clear():
        first[...] = jnp.zeros_like(first)
        second[...] = jnp.zeros_like(second)
        third[...] = jnp.zeros_like(third)

    pl.when(system == 0)(clear)
    low, high, tall = 256, 512, 16 * (kernel_total + 1)

    def part_body(block, blocks):
        wide = blocks * rows
        groups = wide // 16
        c = lax.broadcasted_iota(jnp.int32, (wide, rows), 0) + block * rows
        a = lax.broadcasted_iota(jnp.int32, (wide, rows), 1)
        mask[:wide] = ((c >= col_start) & (a >= row_start)).astype(jnp.bfloat16)

        def put(start, values):
            for group in range(groups):
                stack[group, pl.ds(start, 16), :] = values[group * 16 : group * 16 + 16]

        ones = (
            lax.broadcasted_iota(jnp.int32, (wide, wide), 0)
            == lax.broadcasted_iota(jnp.int32, (wide, wide), 1)
        ).astype(jnp.bfloat16)
        own = jnp.concatenate([science[block + i] for i in range(blocks)], axis=1)
        own = lax.dot_general(ones, own, NT, preferred_element_type=jnp.float32)
        put(kernel_total * 16, own.astype(jnp.bfloat16) * mask[:wide])

        data = jnp.concatenate(
            [jnp.concatenate([window[block + i], window[block + i + 1]], axis=1) for i in range(blocks)], axis=0
        )

        def smooth_chunk(number):
            height = chunk * span
            base = number * height
            lhs = jnp.concatenate(
                [xtab_ref[0, base : base + height, :], xtab_ref[1, base : base + height, :]], axis=1
            )
            out = lax.dot_general(lhs, data, NT, preferred_element_type=jnp.float32).astype(jnp.bfloat16)
            slot = number % 2
            for i in range(blocks):
                smooth[slot, i] = out[:, i * rows : i * rows + rows]

        def basis_chunk(number):
            slot = number % 2
            for place in range(chunk):
                pair = number * chunk + place
                k1, k2 = slice(place * span, place * span + rows), slice(place * span + rows, place * span + span)
                lhs = jnp.concatenate(
                    [jnp.concatenate([smooth[slot, i, k1], smooth[slot, i, k2]], axis=1) for i in range(blocks)],
                    axis=0,
                )
                top = ytab_ref[pair * span : pair * span + rows]
                bottom = ytab_ref[pair * span + rows : pair * span + span]
                blank = jnp.zeros_like(top)
                table = jnp.concatenate(
                    [jnp.concatenate([top, blank], axis=1), jnp.concatenate([blank, bottom], axis=1)], axis=0
                )
                basis = jnp.dot(lhs, table, preferred_element_type=jnp.float32).astype(jnp.bfloat16)
                base = pair * 32 if isinstance(pair, int) else pl.multiple_of(pair * 32, 32)
                put(base, basis[:, :rows] * mask[:wide])
                put(base + 16, basis[:, rows:] * mask[:wide])

        steps = pairs // chunk
        smooth_chunk(0)
        for number in range(steps):
            if number + 1 < steps:
                smooth_chunk(number + 1)
            basis_chunk(number)

        def operand(start, stop):
            return jnp.concatenate([stack[group, start:stop, :] for group in range(groups)], axis=1)

        def gram(lhs, rhs):
            return lax.dot_general(lhs, rhs, NT, preferred_element_type=jnp.float32)

        x0, x1, x2 = operand(0, low), operand(low, high), operand(high, tall)
        second[...] += gram(jnp.concatenate([x0, x1, x2], axis=0), x1)
        first[...] += gram(jnp.concatenate([x0, x2], axis=0), x0)
        third[...] += gram(x2, x2)

    first_block = jnp.minimum(col_start // rows, count - 1)

    @pl.when(first_block % 2 == 1)
    def _():
        part_body(first_block, 1)

    def step(part, carry):
        part_body(2 * part, 2)
        return carry

    lax.fori_loop((first_block + 1) // 2, count // 2, step, 0)

    out_ref[0, 0:32] = fold(first)
    out_ref[0, 32:80] = fold(second)
    out_ref[0, 80:96] = fold(third)
    clear()


CHUNK = 4
VLIM = 24


def normals(bounds, templates, science, tables, half_width):
    owners, systems, half_rows, half_cols = templates.shape
    rows, cols = 2 * half_rows, 2 * half_cols
    span = 2 * rows
    kernel_total = tables[1].shape[0] // 128
    tall = 16 * (kernel_total + 1)
    whole = pl.BlockSpec(memory_space=VMEM)
    return pl.pallas_call(
        functools.partial(normals_kernel, half_width, CHUNK),
        out_shape=jax.ShapeDtypeStruct((systems, 96, 128), jnp.float32),
        grid_spec=pltpu.PrefetchScalarGridSpec(
            num_scalar_prefetch=1,
            grid=(systems,),
            in_specs=[
                whole, whole, whole, whole, whole,
                whole, whole,
            ],
            out_specs=pl.BlockSpec((1, 96, 128), lambda i, s: (i, 0, 0)),
            scratch_shapes=[
                VMEM((cols // 128 + 1, rows, 128), jnp.bfloat16),
                VMEM((cols // 128, rows, 128), jnp.bfloat16),
                VMEM((2, 2, CHUNK * span, rows), jnp.bfloat16),
                VMEM((span // 16, tall, rows), jnp.bfloat16),
                VMEM((span, rows), jnp.bfloat16),
                VMEM((256 + tall - 512, 256), jnp.float32),
                VMEM((tall, 256), jnp.float32),
                VMEM((tall - 512, tall - 512), jnp.float32),
            ],
        ),
        cost_estimate=pl.CostEstimate(flops=12_000_000_000, bytes_accessed=8_000_000, transcendentals=0),
        compiler_params=pltpu.CompilerParams(vmem_limit_bytes=VLIM * 1024 * 1024),
    )(bounds, templates, *science, *tables)


def solve_kernel(kernel_total, pixel_values, even_ref, odd_ref, out_ref):
    systems = 2 * even_ref.shape[0]
    r = lax.broadcasted_iota(jnp.int32, (128, 128), 0)
    l = lax.broadcasted_iota(jnp.int32, (128, 128), 1)
    matrices = []
    for system in range(systems):
        blocks = (odd_ref if system % 2 else even_ref)[system // 2]
        first, second, third = blocks[0:32], blocks[32:80], blocks[80:96]
        zero = jnp.zeros((16, 128), jnp.float32)
        left = jnp.concatenate([first[:16], zero, first[16:32]] + [zero] * 5, axis=0)
        middle = jnp.concatenate([pltpu.roll(second, 16, axis=1)] + [zero] * 5, axis=0)
        right = jnp.concatenate([zero, zero, pltpu.roll(third, 32, axis=1)] + [zero] * 5, axis=0)
        left = jnp.where((l < 16) & ((r < 16) | ((r >= 32) & (r <= kernel_total))), left, 0.0)
        middle = jnp.where((l >= 16) & (l < 32) & (r <= kernel_total), middle, 0.0)
        right = jnp.where((l >= 32) & (l <= kernel_total) & (r >= 32) & (r <= kernel_total), right, 0.0)
        known = left + middle + right
        other = jnp.transpose(known)
        absent = ((r >= 16) & (r < 32) & (l < 16)) | ((l >= 32) & (r < 32))
        whole = jnp.where(absent, other, known) / pixel_values
        whole = whole + jnp.where((r == l) & (r < kernel_total), RIDGE_TERM, 0.0)
        matrices.append(whole[:kernel_total])
    width = kernel_total + 1
    beside = 128 // width
    groups = []
    for start in range(0, systems, beside):
        total = matrices[start]
        for place in range(1, min(beside, systems - start)):
            total = total + pltpu.roll(matrices[start + place], place * width, axis=1)
        groups.append(total)
    row_ids = lax.broadcasted_iota(jnp.int32, (kernel_total, 128), 0)
    base = lax.broadcasted_iota(jnp.int32, (kernel_total, 128), 1) // width * width
    for pivot in range(0, kernel_total, 2):
        place, after = jnp.minimum(base + pivot, 127), jnp.minimum(base + pivot + 1, 127)
        for number, work in enumerate(groups):
            real = base[:1] < min(beside, systems - number * beside) * width
            left, right = jnp.take_along_axis(work, place, axis=1), jnp.take_along_axis(work, after, axis=1)
            top, bottom = work[pivot : pivot + 1], work[pivot + 1 : pivot + 2]
            head = jnp.where(real, left[pivot : pivot + 1], 1.0)
            ratio = right[pivot : pivot + 1] / head
            lower = left[pivot + 1 : pivot + 2]
            top = top / head
            tail = jnp.where(real, right[pivot + 1 : pivot + 2] - lower * ratio, 1.0)
            bottom = (bottom - lower * top) / tail
            top = top - ratio * bottom
            work = work - left * top - right * bottom
            groups[number] = jnp.where(row_ids == pivot, top, jnp.where(row_ids == pivot + 1, bottom, work))
    for number, work in enumerate(groups):
        turned = jnp.transpose(jnp.concatenate([work, jnp.zeros((128 - kernel_total, 128), jnp.float32)], axis=0))
        for place in range(min(beside, systems - number * beside)):
            last = place * width + kernel_total
            out_ref[number * beside + place : number * beside + place + 1] = turned[last : last + 1, :kernel_total]


def solve(even, odd, kernel_total, pixel_values):
    return pl.pallas_call(
        functools.partial(solve_kernel, kernel_total, float(pixel_values)),
        out_shape=jax.ShapeDtypeStruct((2 * even.shape[0], kernel_total), jnp.float32),
        compiler_params=SMALL,
    )(even, odd)


def body(images, partners, coverage, x_filters, row_filters):
    visit = lax.axis_index("visit")
    own_tiles = images[0]
    tile_count, row_count, col_count = own_tiles.shape
    half_width = (x_filters.shape[1] - 1) // 2
    kernel_total = x_filters.shape[0]
    visit_count = partners.shape[0]
    owners = lax.axis_size("tx") * lax.axis_size("ty")
    requests = partners.reshape(visit_count, 2 * tile_count)
    own_requests = lax.dynamic_index_in_dim(requests, visit, 0, keepdims=False)
    share = tile_count // owners
    group = ("tx", "ty")
    sent = send_pack(outgoing_tiles(requests, visit, tile_count), own_tiles)
    arrived = lax.all_to_all(
        sent.reshape((visit_count, CAP) + own_tiles.shape[1:]), "visit", split_axis=0, concat_axis=0, tiled=True
    )
    arrived = arrived.reshape((visit_count * CAP,) + own_tiles.shape[1:])

    blocks = coverage[0]
    block_size = row_count // blocks.shape[2]
    row_blocks = jnp.max(blocks, axis=3).sum(axis=2)
    col_blocks = jnp.max(blocks, axis=2).sum(axis=2)
    counts = jnp.stack([row_blocks, col_blocks], axis=-1).reshape(owners, 2 * share, 2).astype(own_tiles.dtype)
    counts = jnp.pad(counts, ((0, 0), (0, 16 - 2 * share), (0, col_count - 2)))
    science = jnp.concatenate([own_tiles.reshape(owners, share * row_count, col_count), counts], axis=1)
    tx, ty = lax.axis_index("tx"), lax.axis_index("ty")
    parts, row_blocks, col_blocks = [], 0.0, 0.0
    for dx in range(2):
        for dy in range(2):
            peer_x, peer_y = (tx + dx) % 2, (ty + dy) % 2
            part = lax.dynamic_index_in_dim(science, 2 * peer_x + peer_y, 0, keepdims=False)
            if dx or dy:
                swap = 2 * dx + dy
                part = lax.ppermute(part, group, [(i, i ^ swap) for i in range(owners)])
            parts.append(part)
            tally = part[share * row_count : share * row_count + 2 * share, :2].astype(jnp.float32)
            row_blocks += jnp.where(peer_x == 1, tally[:, 0], 0.0)
            col_blocks += jnp.where(peer_y == 1, tally[:, 1], 0.0)
    row_start = 2 * row_count - block_size * row_blocks
    col_start = 2 * col_count - block_size * col_blocks
    bounds = jnp.stack([row_start, col_start], axis=-1).astype(jnp.int32).reshape(share, 2, 2)
    place = jnp.stack([tx, ty]).astype(jnp.int32)

    slots = arrival_slots(own_requests).reshape(tile_count, 2)
    pixel_values = row_count * col_count * owners
    grouped = [group_pack(slots[:, partner], arrived, owners) for partner in range(2)]
    tables = filter_tables(x_filters, row_filters, half_width)
    sums = []
    for partner in range(2):
        templates = lax.all_to_all(grouped[partner], group, split_axis=0, concat_axis=0, tiled=True)
        limits = jnp.concatenate([bounds[:, partner].reshape(-1), place])
        sums.append(normals(limits, templates, parts, tables, half_width))
    coefficients = solve(*sums, kernel_total, pixel_values)
    return coefficients.reshape(1, tile_count // owners, 2, kernel_total)


def solution(mesh):
    return jax.shard_map(
        body,
        mesh=mesh,
        in_specs=(P("visit", None, "ty", "tx"), P(), P("visit", None, None, "ty", "tx"), P(), P()),
        out_specs=P("visit", ("tx", "ty"), None, None),
        check_vma=False,
    )
```

```python
import functools

import jax
import jax.numpy as jnp
from jax import lax
from jax.experimental import pallas as pl
from jax.experimental.pallas import tpu as pltpu
from jax.sharding import PartitionSpec as P

CAP = 2
RIDGE_TERM = 0.002
NT = (((1,), (1,)), ((), ()))
VMEM = pltpu.VMEM
ANY = pl.ANY
SMALL = pltpu.CompilerParams(vmem_limit_bytes=4 * 1024 * 1024)


def outgoing_tiles(requests, sender_visit, tile_count):
    is_sender = (requests == sender_visit).astype(jnp.int32)
    before = jnp.cumsum(is_sender, axis=1) - is_sender
    tile_ids = jnp.arange(2 * tile_count, dtype=jnp.int32)[None, :] // 2
    picked = [
        jnp.sum(jnp.where((is_sender == 1) & (before == slot), tile_ids, 0), axis=1)
        for slot in range(CAP)
    ]
    return jnp.stack(picked, axis=1).reshape(-1)


def arrival_slots(sources):
    count = sources.shape[0]
    same_source = sources[:, None] == sources[None, :]
    earlier = jnp.arange(count)[None, :] < jnp.arange(count)[:, None]
    return sources * CAP + jnp.sum((same_source & earlier).astype(jnp.int32), axis=1)


def send_pack_kernel(index_ref, tiles_ref, out_ref, sems):
    slots = out_ref.shape[0]

    def copy(slot):
        return pltpu.make_async_copy(
            tiles_ref.at[index_ref[slot]], out_ref.at[slot], sems.at[slot]
        )

    for slot in range(slots):
        copy(slot).start()
    for slot in range(slots):
        copy(slot).wait()


def send_pack(indices, tiles):
    slots = indices.shape[0]
    return pl.pallas_call(
        send_pack_kernel,
        out_shape=jax.ShapeDtypeStruct((slots,) + tiles.shape[1:], tiles.dtype),
        grid_spec=pltpu.PrefetchScalarGridSpec(
            num_scalar_prefetch=1,
            grid=(1,),
            in_specs=[pl.BlockSpec(tiles.shape, lambda i, s: (0, 0, 0))],
            out_specs=pl.BlockSpec(memory_space=pltpu.HBM),
            scratch_shapes=[pltpu.SemaphoreType.DMA((slots,))],
        ),
    )(indices, tiles)


def group_pack_kernel(index_ref, arrived_ref, out_ref, sems):
    owners, systems = out_ref.shape[0], out_ref.shape[1]
    started = []
    for owner in range(owners):
        for place in range(systems):
            number = owner * systems + place
            copy = pltpu.make_async_copy(
                arrived_ref.at[index_ref[number]], out_ref.at[owner, place], sems.at[number]
            )
            copy.start()
            started.append(copy)
    for copy in started:
        copy.wait()


def group_pack(indices, arrived, owners):
    count = indices.shape[0]
    shape = (owners, count // owners) + arrived.shape[1:]
    return pl.pallas_call(
        group_pack_kernel,
        out_shape=jax.ShapeDtypeStruct(shape, arrived.dtype),
        grid_spec=pltpu.PrefetchScalarGridSpec(
            num_scalar_prefetch=1,
            grid=(1,),
            in_specs=[pl.BlockSpec(memory_space=ANY)],
            out_specs=pl.BlockSpec(memory_space=pltpu.HBM),
            scratch_shapes=[pltpu.SemaphoreType.DMA((count,))],
        ),
        compiler_params=SMALL,
    )(indices, arrived)


def tables_kernel(half_width, x_ref, y_ref, xtab_ref, ytab_ref):
    height = 128
    r = lax.broadcasted_iota(jnp.int32, (height, 128), 0)
    l = lax.broadcasted_iota(jnp.int32, (height, 128), 1)
    near = jnp.abs(r - l) <= half_width

    def shifted(row):
        return pltpu.roll(jnp.broadcast_to(row, (height, row.shape[1])), 0, axis=1, stride=1, stride_axis=0)

    def body(pair, carry):
        for place in range(2):
            kernel = 2 * pair + place
            rows = pl.ds(pl.multiple_of(kernel * height, height), height)
            table = shifted(x_ref[pl.ds(kernel, 1), :]).astype(jnp.bfloat16)
            xtab_ref[0, rows] = table[:, :128]
            xtab_ref[1, rows] = table[:, 128:]
            table = jnp.where(near, shifted(y_ref[pl.ds(kernel, 1), :]), 0.0).astype(jnp.bfloat16)
            ytab_ref[rows] = table
        return carry

    lax.fori_loop(0, ytab_ref.shape[0] // (2 * height), body, 0)


def pass_kernel(x_ref, y_ref, x_out, y_out):
    x_out[...] = x_ref[...]
    y_out[...] = y_ref[...]


def filter_rows(x_filters, row_filters, half_width):
    kernel_total, taps = x_filters.shape
    x_rows = jnp.pad(x_filters.astype(jnp.float32), ((0, 0), (0, 256 - taps)))
    y_rows = row_filters[:, ::-1].astype(jnp.float32)
    y_rows = jnp.concatenate(
        [y_rows[:, half_width:], jnp.zeros((kernel_total, 128 - taps), jnp.float32), y_rows[:, :half_width]], axis=1
    )
    return pl.pallas_call(
        pass_kernel,
        out_shape=(
            jax.ShapeDtypeStruct(x_rows.shape, jnp.float32),
            jax.ShapeDtypeStruct(y_rows.shape, jnp.float32),
        ),
        cost_estimate=pl.CostEstimate(flops=HINT, bytes_accessed=120_000, transcendentals=0),
        compiler_params=SMALL,
    )(x_rows, y_rows)


HINT = 8_000_000_000


def filter_tables(x_rows, y_rows, half_width):
    kernel_total = x_rows.shape[0]
    return pl.pallas_call(
        functools.partial(tables_kernel, half_width),
        out_shape=(
            jax.ShapeDtypeStruct((2, kernel_total * 128, 128), jnp.bfloat16),
            jax.ShapeDtypeStruct((kernel_total * 128, 128), jnp.bfloat16),
        ),
        compiler_params=pltpu.CompilerParams(vmem_limit_bytes=12 * 1024 * 1024),
    )(x_rows, y_rows)


def lane_tiles(quarter, tile_count):
    tiles = []
    for across in range(2):
        for tile in range(tile_count):
            lanes = slice(tile * 128, tile * 128 + 128)
            tiles.append(jnp.concatenate([quarter(across, 0, lanes), quarter(across, 1, lanes)], axis=0))
    return tiles


def split_dot(lhs, rhs, left):
    value = lhs if left else rhs
    total = None
    for _ in range(3):
        term = value.astype(jnp.bfloat16)
        value = value - term.astype(jnp.float32)
        part = jnp.dot(*((term, rhs) if left else (lhs, term)), preferred_element_type=jnp.float32)
        total = part if total is None else total + part
    return total


def fold(ref):
    height, width = ref.shape
    count = height // 16
    padded = -(-count // 16) * 16
    values = ref[...].reshape(count, 2, 8, width)
    sub = lax.broadcasted_iota(jnp.int32, (count, 8, width), 1)
    lane = lax.broadcasted_iota(jnp.int32, (count, 8, width), 2) % 16
    kept = jnp.where(lane == sub, values[:, 0], jnp.where(lane == sub + 8, values[:, 1], 0.0))
    kept = kept.reshape(count * 8, width)
    r = lax.broadcasted_iota(jnp.int32, (padded, count * 8), 0)
    l = lax.broadcasted_iota(jnp.int32, (padded, count * 8), 1)
    summed = split_dot((l // 8 == r).astype(jnp.bfloat16), kept, False)
    r = lax.broadcasted_iota(jnp.int32, (width, 128), 0)
    l = lax.broadcasted_iota(jnp.int32, (width, 128), 1)
    return split_dot(summed, (r // 16 == l).astype(jnp.bfloat16), True)


def normals_kernel(
    half_width, chunk, bounds_ref, template_ref, near_ref, down_ref, across_ref, far_ref, xtab_ref, ytab_ref,
    out_ref, window, science, smooth, stack, mask, first, second, third,
):
    system = pl.program_id(0)
    row_start, col_start = bounds_ref[2 * system], bounds_ref[2 * system + 1]
    rows = 128
    pairs = ytab_ref.shape[0] // 256
    kernel_total = 2 * pairs
    span = 2 * rows
    half_rows = template_ref.shape[2]
    own_tx, own_ty = bounds_ref[2 * pl.num_programs(0)], bounds_ref[2 * pl.num_programs(0) + 1]

    def template_quarter(tx, ty, lanes):
        return template_ref[2 * tx + ty, system, :, lanes]

    def science_quarter(tx, ty, lanes):
        tile = pl.ds(pl.multiple_of(system * half_rows, half_rows), half_rows)
        same = jnp.where(own_ty == ty, near_ref[tile, lanes], down_ref[tile, lanes])
        other = jnp.where(own_ty == ty, across_ref[tile, lanes], far_ref[tile, lanes])
        return jnp.where(own_tx == tx, same, other)

    tiles = lane_tiles(template_quarter, template_ref.shape[3] // 128)
    count = len(tiles)
    lane = lax.broadcasted_iota(jnp.int32, (rows, 128), 1)
    rolled = [pltpu.roll(tile.astype(jnp.float32), half_width, axis=1) for tile in tiles]
    zero = jnp.zeros((rows, 128), jnp.float32)
    for place in range(count + 1):
        before = rolled[place - 1] if place > 0 else zero
        here = rolled[place] if place < count else zero
        window[place] = jnp.where(lane < half_width, before, here).astype(jnp.bfloat16)
    for place, tile in enumerate(lane_tiles(science_quarter, template_ref.shape[3] // 128)):
        science[place] = tile

    def clear():
        first[...] = jnp.zeros_like(first)
        second[...] = jnp.zeros_like(second)
        third[...] = jnp.zeros_like(third)

    pl.when(system == 0)(clear)
    low, high, tall = 256, 512, 16 * (kernel_total + 1)

    def part_body(block, blocks):
        wide = blocks * rows
        groups = wide // 16
        c = lax.broadcasted_iota(jnp.int32, (wide, rows), 0) + block * rows
        a = lax.broadcasted_iota(jnp.int32, (wide, rows), 1)
        mask[:wide] = ((c >= col_start) & (a >= row_start)).astype(jnp.bfloat16)

        def put(start, values):
            for group in range(groups):
                stack[group, pl.ds(start, 16), :] = values[group * 16 : group * 16 + 16]

        ones = (
            lax.broadcasted_iota(jnp.int32, (wide, wide), 0)
            == lax.broadcasted_iota(jnp.int32, (wide, wide), 1)
        ).astype(jnp.bfloat16)
        own = jnp.concatenate([science[block + i] for i in range(blocks)], axis=1)
        own = lax.dot_general(ones, own, NT, preferred_element_type=jnp.float32)
        put(kernel_total * 16, own.astype(jnp.bfloat16) * mask[:wide])

        data = jnp.concatenate(
            [jnp.concatenate([window[block + i], window[block + i + 1]], axis=1) for i in range(blocks)], axis=0
        )

        def smooth_chunk(number):
            height = chunk * span
            base = number * height
            lhs = jnp.concatenate(
                [xtab_ref[0, base : base + height, :], xtab_ref[1, base : base + height, :]], axis=1
            )
            out = lax.dot_general(lhs, data, NT, preferred_element_type=jnp.float32).astype(jnp.bfloat16)
            slot = number % 2
            for i in range(blocks):
                smooth[slot, i] = out[:, i * rows : i * rows + rows]

        def basis_chunk(number):
            slot = number % 2
            for place in range(chunk):
                pair = number * chunk + place
                k1, k2 = slice(place * span, place * span + rows), slice(place * span + rows, place * span + span)
                lhs = jnp.concatenate(
                    [jnp.concatenate([smooth[slot, i, k1], smooth[slot, i, k2]], axis=1) for i in range(blocks)],
                    axis=0,
                )
                top = ytab_ref[pair * span : pair * span + rows]
                bottom = ytab_ref[pair * span + rows : pair * span + span]
                blank = jnp.zeros_like(top)
                table = jnp.concatenate(
                    [jnp.concatenate([top, blank], axis=1), jnp.concatenate([blank, bottom], axis=1)], axis=0
                )
                basis = jnp.dot(lhs, table, preferred_element_type=jnp.float32).astype(jnp.bfloat16)
                base = pair * 32 if isinstance(pair, int) else pl.multiple_of(pair * 32, 32)
                put(base, basis[:, :rows] * mask[:wide])
                put(base + 16, basis[:, rows:] * mask[:wide])

        steps = pairs // chunk
        smooth_chunk(0)
        for number in range(steps):
            if number + 1 < steps:
                smooth_chunk(number + 1)
            basis_chunk(number)

        def operand(start, stop):
            return jnp.concatenate([stack[group, start:stop, :] for group in range(groups)], axis=1)

        def gram(lhs, rhs):
            return lax.dot_general(lhs, rhs, NT, preferred_element_type=jnp.float32)

        x0, x1, x2 = operand(0, low), operand(low, high), operand(high, tall)
        second[...] += gram(jnp.concatenate([x0, x1, x2], axis=0), x1)
        first[...] += gram(jnp.concatenate([x0, x2], axis=0), x0)
        third[...] += gram(x2, x2)

    first_block = jnp.minimum(col_start // rows, count - 1)

    @pl.when(first_block % 2 == 1)
    def _():
        part_body(first_block, 1)

    def step(part, carry):
        part_body(2 * part, 2)
        return carry

    lax.fori_loop((first_block + 1) // 2, count // 2, step, 0)

    out_ref[0, 0:32] = fold(first)
    out_ref[0, 32:80] = fold(second)
    out_ref[0, 80:96] = fold(third)
    clear()


CHUNK = 4
VLIM = 24


def normals(bounds, templates, science, tables, half_width):
    owners, systems, half_rows, half_cols = templates.shape
    rows, cols = 2 * half_rows, 2 * half_cols
    span = 2 * rows
    kernel_total = tables[1].shape[0] // 128
    tall = 16 * (kernel_total + 1)
    whole = pl.BlockSpec(memory_space=VMEM)
    return pl.pallas_call(
        functools.partial(normals_kernel, half_width, CHUNK),
        out_shape=jax.ShapeDtypeStruct((systems, 96, 128), jnp.float32),
        grid_spec=pltpu.PrefetchScalarGridSpec(
            num_scalar_prefetch=1,
            grid=(systems,),
            in_specs=[
                whole, whole, whole, whole, whole,
                whole, whole,
            ],
            out_specs=pl.BlockSpec((1, 96, 128), lambda i, s: (i, 0, 0)),
            scratch_shapes=[
                VMEM((cols // 128 + 1, rows, 128), jnp.bfloat16),
                VMEM((cols // 128, rows, 128), jnp.bfloat16),
                VMEM((2, 2, CHUNK * span, rows), jnp.bfloat16),
                VMEM((span // 16, tall, rows), jnp.bfloat16),
                VMEM((span, rows), jnp.bfloat16),
                VMEM((256 + tall - 512, 256), jnp.float32),
                VMEM((tall, 256), jnp.float32),
                VMEM((tall - 512, tall - 512), jnp.float32),
            ],
        ),
        cost_estimate=pl.CostEstimate(flops=12_000_000_000, bytes_accessed=8_000_000, transcendentals=0),
        compiler_params=pltpu.CompilerParams(vmem_limit_bytes=VLIM * 1024 * 1024),
    )(bounds, templates, *science, *tables)


def solve_kernel(kernel_total, pixel_values, even_ref, odd_ref, out_ref):
    systems = 2 * even_ref.shape[0]
    r = lax.broadcasted_iota(jnp.int32, (128, 128), 0)
    l = lax.broadcasted_iota(jnp.int32, (128, 128), 1)
    matrices = []
    for system in range(systems):
        blocks = (odd_ref if system % 2 else even_ref)[system // 2]
        first, second, third = blocks[0:32], blocks[32:80], blocks[80:96]
        zero = jnp.zeros((16, 128), jnp.float32)
        left = jnp.concatenate([first[:16], zero, first[16:32]] + [zero] * 5, axis=0)
        middle = jnp.concatenate([pltpu.roll(second, 16, axis=1)] + [zero] * 5, axis=0)
        right = jnp.concatenate([zero, zero, pltpu.roll(third, 32, axis=1)] + [zero] * 5, axis=0)
        left = jnp.where((l < 16) & ((r < 16) | ((r >= 32) & (r <= kernel_total))), left, 0.0)
        middle = jnp.where((l >= 16) & (l < 32) & (r <= kernel_total), middle, 0.0)
        right = jnp.where((l >= 32) & (l <= kernel_total) & (r >= 32) & (r <= kernel_total), right, 0.0)
        known = left + middle + right
        other = jnp.transpose(known)
        absent = ((r >= 16) & (r < 32) & (l < 16)) | ((l >= 32) & (r < 32))
        whole = jnp.where(absent, other, known) / pixel_values
        whole = whole + jnp.where((r == l) & (r < kernel_total), RIDGE_TERM, 0.0)
        matrices.append(whole[:kernel_total])
    width = kernel_total + 1
    beside = 128 // width
    groups = []
    for start in range(0, systems, beside):
        total = matrices[start]
        for place in range(1, min(beside, systems - start)):
            total = total + pltpu.roll(matrices[start + place], place * width, axis=1)
        groups.append(total)
    row_ids = lax.broadcasted_iota(jnp.int32, (kernel_total, 128), 0)
    base = lax.broadcasted_iota(jnp.int32, (kernel_total, 128), 1) // width * width
    for pivot in range(0, kernel_total, 2):
        place, after = jnp.minimum(base + pivot, 127), jnp.minimum(base + pivot + 1, 127)
        for number, work in enumerate(groups):
            real = base[:1] < min(beside, systems - number * beside) * width
            left, right = jnp.take_along_axis(work, place, axis=1), jnp.take_along_axis(work, after, axis=1)
            top, bottom = work[pivot : pivot + 1], work[pivot + 1 : pivot + 2]
            head = jnp.where(real, left[pivot : pivot + 1], 1.0)
            ratio = right[pivot : pivot + 1] / head
            lower = left[pivot + 1 : pivot + 2]
            top = top / head
            tail = jnp.where(real, right[pivot + 1 : pivot + 2] - lower * ratio, 1.0)
            bottom = (bottom - lower * top) / tail
            top = top - ratio * bottom
            work = work - left * top - right * bottom
            groups[number] = jnp.where(row_ids == pivot, top, jnp.where(row_ids == pivot + 1, bottom, work))
    for number, work in enumerate(groups):
        turned = jnp.transpose(jnp.concatenate([work, jnp.zeros((128 - kernel_total, 128), jnp.float32)], axis=0))
        for place in range(min(beside, systems - number * beside)):
            last = place * width + kernel_total
            out_ref[number * beside + place : number * beside + place + 1] = turned[last : last + 1, :kernel_total]


def solve(even, odd, kernel_total, pixel_values):
    return pl.pallas_call(
        functools.partial(solve_kernel, kernel_total, float(pixel_values)),
        out_shape=jax.ShapeDtypeStruct((2 * even.shape[0], kernel_total), jnp.float32),
        compiler_params=SMALL,
    )(even, odd)


def body(images, partners, coverage, x_filters, row_filters):
    visit = lax.axis_index("visit")
    own_tiles = images[0]
    tile_count, row_count, col_count = own_tiles.shape
    half_width = (x_filters.shape[1] - 1) // 2
    kernel_total = x_filters.shape[0]
    visit_count = partners.shape[0]
    owners = lax.axis_size("tx") * lax.axis_size("ty")
    requests = partners.reshape(visit_count, 2 * tile_count)
    own_requests = lax.dynamic_index_in_dim(requests, visit, 0, keepdims=False)
    share = tile_count // owners
    group = ("tx", "ty")
    sent = send_pack(outgoing_tiles(requests, visit, tile_count), own_tiles)
    arrived = lax.all_to_all(
        sent.reshape((visit_count, CAP) + own_tiles.shape[1:]), "visit", split_axis=0, concat_axis=0, tiled=True
    )
    arrived = arrived.reshape((visit_count * CAP,) + own_tiles.shape[1:])

    blocks = coverage[0]
    block_size = row_count // blocks.shape[2]
    row_blocks = jnp.max(blocks, axis=3).sum(axis=2)
    col_blocks = jnp.max(blocks, axis=2).sum(axis=2)
    counts = jnp.stack([row_blocks, col_blocks], axis=-1).reshape(owners, 2 * share, 2).astype(own_tiles.dtype)
    counts = jnp.pad(counts, ((0, 0), (0, 16 - 2 * share), (0, col_count - 2)))
    science = jnp.concatenate([own_tiles.reshape(owners, share * row_count, col_count), counts], axis=1)
    tx, ty = lax.axis_index("tx"), lax.axis_index("ty")
    parts, row_blocks, col_blocks = [], 0.0, 0.0
    for dx in range(2):
        for dy in range(2):
            peer_x, peer_y = (tx + dx) % 2, (ty + dy) % 2
            part = lax.dynamic_index_in_dim(science, 2 * peer_x + peer_y, 0, keepdims=False)
            if dx or dy:
                swap = 2 * dx + dy
                part = lax.ppermute(part, group, [(i, i ^ swap) for i in range(owners)])
            parts.append(part)
            tally = part[share * row_count : share * row_count + 2 * share, :2].astype(jnp.float32)
            row_blocks += jnp.where(peer_x == 1, tally[:, 0], 0.0)
            col_blocks += jnp.where(peer_y == 1, tally[:, 1], 0.0)
    row_start = 2 * row_count - block_size * row_blocks
    col_start = 2 * col_count - block_size * col_blocks
    bounds = jnp.stack([row_start, col_start], axis=-1).astype(jnp.int32).reshape(share, 2, 2)
    place = jnp.stack([tx, ty]).astype(jnp.int32)

    slots = arrival_slots(own_requests).reshape(tile_count, 2)
    pixel_values = row_count * col_count * owners
    grouped = [group_pack(slots[:, partner], arrived, owners) for partner in range(2)]
    filters = filter_rows(x_filters, row_filters, half_width)
    *filters, _ = lax.optimization_barrier((*filters, grouped[0]))
    tables = filter_tables(*filters, half_width)
    sums = []
    for partner in range(2):
        templates = lax.all_to_all(grouped[partner], group, split_axis=0, concat_axis=0, tiled=True)
        limits = jnp.concatenate([bounds[:, partner].reshape(-1), place])
        sums.append(normals(limits, templates, parts, tables, half_width))
    coefficients = solve(*sums, kernel_total, pixel_values)
    return coefficients.reshape(1, tile_count // owners, 2, kernel_total)


def solution(mesh):
    return jax.shard_map(
        body,
        mesh=mesh,
        in_specs=(P("visit", None, "ty", "tx"), P(), P("visit", None, None, "ty", "tx"), P(), P()),
        out_specs=P("visit", ("tx", "ty"), None, None),
        check_vma=False,
    )
```
